1024 devices in a mesh: gx: 32 (over y, z_hi, core), gy: 32 (over z_lo, x).
Axes of the slice: x: 4, y: 4, z: 32 (z_hi: 4, z_lo: 8; z = z_hi * 8 + z_lo), core: 2. Of those that a mesh axis runs over, the one named last changes fastest.
Arguments:
- right_sides: float32 [16, 4, 128, 4096], P(None, None, 'gx', 'gy'), may hold values from -12 to 12, as said below
- coefficients: float32 [27, 4, 128, 4096], P(None, None, 'gx', 'gy'), may hold values from -0.045 to 2, as said below
Outputs:
- basis_q: float32 [80, 4, 128, 4096], P(None, None, 'gx', 'gy')
- factor_r: float32 [80, 80], replicated
The draws below stay inside these ranges and needn't reach their ends.
Inputs may be any that keep to these rules, and one draw needn't show every extreme that they name: `right_sides`: each entry is the product of a value of order one and a factor that grows from 1 to 3 along x. `coefficients`: the centre coefficient (index 13) lies in 1 to 2, the other 26 in -0.045 to 0.015.
All inputs are finite; a program needn't handle non-finite values.
Results may differ from the reference program's by a relative error of at most 0.0003.
Values sent between devices are 32-bit elements; how exact they have to be, the bound alone decides.
No kernel may reach another device: no remote copies, remote signals or barrier semaphores. Data moves between devices by JAX's collectives and lax.ppermute only.
A program may use at most 32 MiB of HBM per device.

```python
import jax
import jax.numpy as jnp
from jax import lax

RHS = 16
STEPS = 4
NX = 128
NY = 4096
NZ = 4


def draw_right_sides(key, part):
    ramp = jnp.power(jnp.float32(3.0), jnp.arange(NX, dtype=jnp.float32) / jnp.float32(NX - 1))
    values = jnp.clip(jax.random.normal(key, (RHS, NZ, NX, NY), jnp.float32), -4.0, 4.0)
    return values * ramp[None, None, :, None]


def draw_coefficients(key, part):
    first = jax.random.uniform(jax.random.fold_in(key, 1), (27, NZ, NX, NY), jnp.float32)
    second = jax.random.uniform(jax.random.fold_in(key, 2), (27, NZ, NX, NY), jnp.float32)
    others = -0.03 * first + 0.015 * (2.0 * second - 1.0)
    middle = 1.0 + second[13]
    marker = (jnp.arange(27) == 13)[:, None, None, None]
    return jnp.where(marker, middle[None], others)


def setup_inputs(seed: int = 0) -> dict:
    key_of = jax.random.split(jax.random.key(seed), 3)
    right_sides = draw_right_sides(jax.random.fold_in(key_of[2], 71), 0)
    coefficients = draw_coefficients(jax.random.fold_in(key_of[2], 71), 0)
    return {"right_sides": right_sides, "coefficients": coefficients}


OFFSETS = tuple(((plane_step, row_step, col_step) for plane_step in (-1, 0, 1) for row_step in (-1, 0, 1) for col_step in (-1, 0, 1)))
CENTER_SHIFT = 1.5
HALF_SPAN = 0.5

def apply_operator(padded, coefficients):
    planes, rows, columns = (coefficients.shape[1], coefficients.shape[2], coefficients.shape[3])
    result = jnp.zeros((padded.shape[0], planes, rows, columns), jnp.float32)
    for number, (plane_step, row_step, col_step) in enumerate(OFFSETS):
        window = padded[:, 1 + plane_step:1 + plane_step + planes, 1 + row_step:1 + row_step + rows, 1 + col_step:1 + col_step + columns]
        result = result + coefficients[number][None] * window
    return result

def chebyshev_next(padded, coefficients, previous):
    center = padded[:, 1:-1, 1:-1, 1:-1]
    shifted = (apply_operator(padded, coefficients) - CENTER_SHIFT * center) / HALF_SPAN
    if previous is None:
        return shifted
    return 2.0 * shifted - previous

def pad_grid(vectors):
    wrapped = jnp.pad(vectors, ((0, 0), (0, 0), (1, 1), (0, 0)), mode='wrap')
    return jnp.pad(wrapped, ((0, 0), (1, 1), (0, 0), (1, 1)))

def reference(right_sides, coefficients):
    blocks = [right_sides]
    previous = None
    current = right_sides
    for step in range(STEPS):
        following = chebyshev_next(pad_grid(current), coefficients, previous)
        previous, current = (current, following)
        blocks.append(current)
    stacked = jnp.concatenate(blocks, axis=0)
    flat = stacked.reshape(stacked.shape[0], -1)
    gram = jnp.dot(flat, flat.T, precision=lax.Precision.HIGHEST) / jnp.float32(flat.shape[1])
    factor_lower = jnp.linalg.cholesky(gram)
    identity = jnp.eye(flat.shape[0], dtype=jnp.float32)
    inverse = jax.scipy.linalg.solve_triangular(factor_lower, identity, lower=True)
    solved = jnp.dot(inverse, flat, precision=lax.Precision.HIGHEST)
    return (solved.reshape(stacked.shape), factor_lower.T)
```

```python
import jax
import jax.numpy as jnp
from jax import lax
from jax.sharding import Mesh, PartitionSpec as P

STEPS = 4


OFFSETS = tuple(
    (
        (plane_step, row_step, col_step)
        for plane_step in (-1, 0, 1)
        for row_step in (-1, 0, 1)
        for col_step in (-1, 0, 1)
    )
)
CENTER_SHIFT = 1.5
HALF_SPAN = 0.5


def padded_2(array, sides, width):
    for axis, dim in sides:
        devices, length = (lax.axis_size(axis), array.shape[dim])
        up = [(i, (i + 1) % devices) for i in range(devices)]
        down = [(j, i) for i, j in up]
        last = lax.slice_in_dim(array, length - width, length, axis=dim)
        leading = lax.slice_in_dim(array, 0, width, axis=dim)
        before = lax.ppermute(last, axis, up)
        after = lax.ppermute(leading, axis, down)
        array = jnp.concatenate([before, array, after], axis=dim)
    return array


def apply_operator(padded, coefficients):
    planes, rows, columns = (coefficients.shape[1], coefficients.shape[2], coefficients.shape[3])
    result = jnp.zeros((padded.shape[0], planes, rows, columns), jnp.float32)
    for number, (plane_step, row_step, col_step) in enumerate(OFFSETS):
        window = padded[
            :,
            1 + plane_step : 1 + plane_step + planes,
            1 + row_step : 1 + row_step + rows,
            1 + col_step : 1 + col_step + columns,
        ]
        result = result + coefficients[number][None] * window
    return result


def chebyshev_next(padded, coefficients, previous):
    center = padded[:, 1:-1, 1:-1, 1:-1]
    shifted = (apply_operator(padded, coefficients) - CENTER_SHIFT * center) / HALF_SPAN
    if previous is None:
        return shifted
    return 2.0 * shifted - previous


def trim_edges(ghosted, margin):
    extent = ghosted.shape[-1]
    places = jnp.arange(extent)
    column = lax.axis_index(GY)
    last_column = lax.axis_size(GY) - 1
    outside = (column == 0) & (places < margin) | (column == last_column) & (
        places >= extent - margin
    )
    inside = jnp.logical_not(outside).astype(ghosted.dtype)
    return ghosted * inside


def pad_planes(ghosted):
    return jnp.pad(ghosted, ((0, 0), (1, 1), (0, 0), (0, 0)))


PLANE = ("y", "c", "x")
COLUMN = ("zh", "zl")
GX = ("y", "zh", "c")
GY = ("zl", "x")


def exchange(pieces, axes):
    return lax.all_to_all(pieces, axes, split_axis=0, concat_axis=0, tiled=True)


def summed_everywhere(local_gram):
    flat = jnp.pad(local_gram.reshape(-1), (0, 32 * 256 - local_gram.size)).reshape(32, 256)
    piece = exchange(flat, PLANE).sum(axis=0)
    piece = exchange(jnp.broadcast_to(piece, (32, 256)), COLUMN).sum(axis=0)
    whole = exchange(jnp.broadcast_to(piece, (32, 256)), PLANE)
    return whole.reshape(-1)[: local_gram.size].reshape(local_gram.shape)


def local(right_sides, coefficients):
    blocks = [right_sides]
    previous = None
    current = right_sides
    for step in range(STEPS):
        ghosted = padded_2(current, ((GX, 2), (GY, 3)), 1)
        ghosted = trim_edges(ghosted, 1)
        following = chebyshev_next(pad_planes(ghosted), coefficients, previous)
        previous, current = (current, following)
        blocks.append(current)
    stacked = jnp.concatenate(blocks, axis=0)
    flat = stacked.reshape(stacked.shape[0], -1)
    local_gram = jnp.dot(flat, flat.T, precision=lax.Precision.HIGHEST)
    gram_sum = summed_everywhere(local_gram)
    total_cells = flat.shape[1] * lax.axis_size(GX) * lax.axis_size(GY)
    gram = gram_sum / jnp.float32(total_cells)
    factor_lower = jnp.linalg.cholesky(gram)
    identity = jnp.eye(flat.shape[0], dtype=jnp.float32)
    inverse = jax.scipy.linalg.solve_triangular(factor_lower, identity, lower=True)
    solved = jnp.dot(inverse, flat, precision=lax.Precision.HIGHEST)
    return (solved.reshape(stacked.shape), factor_lower.T)


def solution(mesh):
    mesh = Mesh(mesh.devices.reshape(4, 4, 2, 8, 4), ("y", "zh", "c", "zl", "x"))
    placed = (P(None, None, GX, GY), P(None, None, GX, GY))
    return jax.shard_map(
        local,
        mesh=mesh,
        in_specs=placed,
        out_specs=(P(None, None, GX, GY), P()),
        check_vma=False,
    )
```

```python
import functools

import jax
import jax.numpy as jnp
from jax import lax
from jax.experimental import pallas as pl
from jax.experimental.pallas import tpu as pltpu
from jax.sharding import Mesh, PartitionSpec as P

STEPS = 4
RHS = 16
WIDTH = RHS * (STEPS + 1)
ROWS = 4
PLANES = 4
LANES = 128
CELLS = ROWS * PLANES
REACH = STEPS

PLANE = ("y", "c", "x")
COLUMN = ("zh", "zl")
GX = ("y", "zh", "c")
GY = ("zl", "x")

FIRST_K = (0 + 9, 0, 0, 0)
LAST_K = (27, 27, 27, 18)
PLANE_AT = (0, 18, 45, 72)
PER_ROW = 96
VECTOR_ROWS = RHS * CELLS
COEF_ROWS = ROWS * PER_ROW
SENT_COEFS = (ROWS - 1) * PER_ROW
EDGE_ROWS = 24
MESSAGE = VECTOR_ROWS + SENT_COEFS + 2 * EDGE_ROWS
VECTOR_GROUPS = VECTOR_ROWS // 8
COEF_GROUPS = COEF_ROWS // 8
EXTENT = ROWS + 2 * REACH

F32 = jnp.float32
BF16 = jnp.bfloat16


def lane_index(shape):
    return lax.broadcasted_iota(jnp.int32, shape, 1)


def spread(weights, x, end, row):
    return weights[x, end, pl.ds(row, 8, stride=0), :]


def prepare_kernel(v_ref, c_ref, coefs_ref, up_ref, down_ref):
    for x in range(ROWS):
        for z in range(PLANES):
            first, count = FIRST_K[z], LAST_K[z] - FIRST_K[z]
            rows = c_ref[pl.ds(first * CELLS + z * ROWS + x, count, stride=CELLS), :]
            number = first + lax.broadcasted_iota(jnp.int32, rows.shape, 0)
            rows = jnp.where(number == 13, 4.0 * rows - 6.0, 4.0 * rows)
            at = x * PER_ROW + PLANE_AT[z]
            coefs_ref[at : at + count, :] = rows
        at = x * PER_ROW + 90
        coefs_ref[at : at + 6, :] = jnp.zeros((6, LANES), F32)
    slot = lane_index((8, LANES)) // 4
    zero = jnp.zeros((8, LANES), F32)
    up, down = [zero] * 3, [zero] * 3
    for group in range(VECTOR_GROUPS + COEF_GROUPS):
        if group < VECTOR_GROUPS:
            block = v_ref[8 * group : 8 * group + 8, :]
        else:
            at = 8 * (group - VECTOR_GROUPS)
            block = coefs_ref[at : at + 8, :]
        pack, place = divmod(group, 32)
        here = slot == place
        up[pack] = jnp.where(here, pltpu.roll(block, (4 * place + 4) % LANES, 1), up[pack])
        down[pack] = jnp.where(here, pltpu.roll(block, (4 * place) % LANES, 1), down[pack])
    for pack in range(3):
        up_ref[8 * pack : 8 * pack + 8, :] = up[pack]
        down_ref[8 * pack : 8 * pack + 8, :] = down[pack]


def message_kernel(v_ref, coefs_ref, low_ref, high_ref, near_ref, far_ref):
    core = lax.axis_index("c")
    for ref, skip in ((near_ref, 1 - core), (far_ref, core)):
        start = pl.multiple_of(skip * PER_ROW, 8)
        ref[0:VECTOR_ROWS, :] = v_ref[...]
        ref[VECTOR_ROWS : VECTOR_ROWS + SENT_COEFS, :] = coefs_ref[pl.ds(start, SENT_COEFS), :]
        at = VECTOR_ROWS + SENT_COEFS
        ref[at : at + EDGE_ROWS, :] = low_ref[...]
        ref[at + EDGE_ROWS : at + 2 * EDGE_ROWS, :] = high_ref[...]


def basis_kernel(
    v_ref, coefs_ref, low_ref, high_ref, near_ref, far_ref,
    high_part_ref, low_part_ref, packed_ref,
    sides, flat, basis, shifted, weights, stacked, gram,
):
    core = lax.axis_index("c")
    lane = lane_index((8, LANES))
    wide = lane_index((RHS, LANES))

    @pl.when(core == 0)
    def _():
        sides[0] = far_ref[...]
        sides[1] = near_ref[...]

    @pl.when(core != 0)
    def _():
        sides[0] = near_ref[...]
        sides[1] = far_ref[...]

    def both_ends(block, group, low, high):
        pack, place = divmod(group, 32)
        back = pltpu.roll(low[pack], (-(4 * place + 4)) % LANES, 1)
        left = jnp.where(lane >= LANES - 4, back, block)
        back = pltpu.roll(high[pack], (-(4 * place)) % LANES, 1)
        right = jnp.where(lane < 4, back, block)
        return left, right

    def put(step, x, z, end, value):
        basis[step, x, z, end] = value
        if step < STEPS:
            shifted[0, x, z, end] = pltpu.roll(value, 1, 1)
            shifted[1, x, z, end] = pltpu.roll(value, LANES - 1, 1)

    at = VECTOR_ROWS + SENT_COEFS
    for tile in range(3):
        if tile == 1:
            vectors, coefs = v_ref, coefs_ref
            low = [low_ref[8 * p : 8 * p + 8, :] for p in range(3)]
            high = [high_ref[8 * p : 8 * p + 8, :] for p in range(3)]
            first_row, rows, skip = ROWS + REACH - ROWS, ROWS, 0
        else:
            side = sides.at[tile // 2]
            vectors, coefs = side, side.at[pl.ds(VECTOR_ROWS, SENT_COEFS)]
            low = [side[at + 8 * p : at + 8 * p + 8, :] for p in range(3)]
            high = [side[at + EDGE_ROWS + 8 * p : at + EDGE_ROWS + 8 * p + 8, :] for p in range(3)]
            first_row, rows = (0, ROWS - 1) if tile == 0 else (ROWS + REACH, ROWS - 1)
            skip = 1 if tile == 0 else 0
        for group in range(VECTOR_GROUPS):
            block = vectors[8 * group : 8 * group + 8, :]
            left, right = both_ends(block, group, low, high)
            flat[0, 8 * group : 8 * group + 8, :] = left
            flat[1, 8 * group : 8 * group + 8, :] = right
        for x in range(ROWS):
            for z in range(PLANES):
                for end in range(2):
                    value = flat[end, pl.ds(z * ROWS + x, RHS, stride=CELLS), :]
                    put(0, first_row + x, z, end, value)
        for x in range(rows):
            row = first_row + skip + x - 1
            for part in range(PER_ROW // 8):
                block = coefs[x * PER_ROW + 8 * part : x * PER_ROW + 8 * part + 8, :]
                group = VECTOR_GROUPS + (x + skip) * (PER_ROW // 8) + part
                left, right = both_ends(block, group, low, high)
                weights[row, 0, 8 * part : 8 * part + 8, :] = left
                weights[row, 1, 8 * part : 8 * part + 8, :] = right

    for step in range(1, STEPS + 1):
        first, last = step, EXTENT - step

        def one_row(x, _, step=step):
            for end in range(2):
                total = [None] * PLANES
                for dx in range(-1, 2):
                    for dy in range(-1, 2):
                        for source in range(PLANES):
                            if dy == 0:
                                value = basis[step - 1, x + dx, source, end]
                            else:
                                value = shifted[(dy + 1) // 2, x + dx, source, end]
                            for dz in range(-1, 2):
                                z = source - dz
                                if not 0 <= z < PLANES:
                                    continue
                                k = 9 * (dz + 1) + 3 * (dx + 1) + (dy + 1)
                                row = PLANE_AT[z] + k - FIRST_K[z]
                                weight = spread(weights, x - 1, end, row)
                                term = jnp.concatenate([weight, weight], axis=0) * value
                                total[z] = term if total[z] is None else total[z] + term
                for z in range(PLANES):
                    if step == 1:
                        total[z] = 0.5 * total[z]
                    else:
                        total[z] = total[z] - basis[step - 2, x, z, end]
                    basis[step, x, z, end] = total[z]
            return 0

        lax.fori_loop(first, last, one_row, 0)

        if step < STEPS:

            def shift_row(x, _, step=step):
                for end in range(2):
                    for z in range(PLANES):
                        value = basis[step, x, z, end]
                        shifted[0, x, z, end] = pltpu.roll(value, 1, 1)
                        shifted[1, x, z, end] = pltpu.roll(value, LANES - 1, 1)
                return 0

            lax.fori_loop(first, last, shift_row, 0)

    for step in range(STEPS + 1):
        for x in range(ROWS):
            for z in range(PLANES):
                left = basis[step, REACH + x, z, 0]
                right = basis[step, REACH + x, z, 1]
                value = jnp.where(wide < LANES // 2, left, right)
                rest = value - value.astype(BF16).astype(F32)
                cell = (z * ROWS + x) * LANES
                high_part_ref[RHS * step : RHS * step + RHS, cell : cell + LANES] = value.astype(BF16)
                low_part_ref[RHS * step : RHS * step + RHS, cell : cell + LANES] = rest.astype(BF16)

    dims = (((1,), (1,)), ((), ()))
    top, rest = high_part_ref[...], low_part_ref[...]
    main = lax.dot_general(top, top, dims, preferred_element_type=F32)
    cross = lax.dot_general(rest, top, dims, preferred_element_type=F32)
    mirror = lax.dot_general(top, rest, dims, preferred_element_type=F32)
    gram[:, 0:WIDTH] = main + (cross + mirror)
    lane32 = lane_index((32, LANES))
    packed = jnp.where(lane32 < WIDTH, gram[48:80, :], pltpu.roll(gram[16:48, :], WIDTH, 1))
    packed_ref[...] = packed
    packed_ref[0:16, :] = jnp.where(wide < 112, packed[0:16, :], pltpu.roll(gram[0:16, :], 112, 1))


def finish_kernel(cells, packed_ref, high_ref, low_ref, q_ref, r_ref, square):
    packed = packed_ref[...] * (1.0 / cells)
    square[...] = jnp.zeros((LANES, LANES), F32)
    square[48:80, :] = packed
    square[16:48, :] = pltpu.roll(packed, 48, 1)
    square[0:16, :] = pltpu.roll(packed[0:16, :], 16, 1)
    whole = square[...]
    turned = whole.T
    row = lax.broadcasted_iota(jnp.int32, (LANES, LANES), 0)
    lane = lane_index((LANES, LANES))
    square[...] = jnp.where(lane <= row, whole, turned)
    lane = lane_index((8, LANES))
    inner = lax.broadcasted_iota(jnp.int32, (8, LANES), 0)
    groups = WIDTH // 8
    part = [square[8 * g : 8 * g + 8, :] for g in range(groups)]
    for j in range(WIDTH):
        own, place = divmod(j, 8)
        pivot_row = jnp.broadcast_to(part[own][place : place + 1, :], (8, LANES))
        pivot = jnp.broadcast_to(pivot_row[:, j : j + 1], (8, LANES))
        here = lane == j
        scaled = jnp.where(here, 1.0, pivot_row) * (1.0 / pivot)
        for g in range(own, groups):
            column = jnp.broadcast_to(part[g][:, j : j + 1], (8, LANES))
            new = jnp.where(here, 0.0, part[g]) - column * scaled
            part[g] = jnp.where(inner > place, new, part[g]) if g == own else new
    for g in range(groups):
        diagonal = lane == inner + 8 * g
        pivots = jnp.sum(jnp.where(diagonal, part[g], 0.0), axis=1, keepdims=True)
        scale = jnp.broadcast_to(lax.rsqrt(pivots), (8, LANES))
        r_ref[8 * g : 8 * g + 8, :] = jnp.where(lane >= inner + 8 * g, part[g] * scale, 0.0)[:, 0:WIDTH]
        lower = jnp.where(diagonal, scale, part[g] * scale)
        square[8 * g : 8 * g + 8, :] = jnp.where(lane <= inner + 8 * g, lower, 0.0)
    inverse = square[0:WIDTH, 0:WIDTH]
    top = inverse.astype(BF16)
    rest = (inverse - top.astype(F32)).astype(BF16)
    for cell in range(CELLS):
        at = slice(cell * LANES, cell * LANES + LANES)
        high, low = high_ref[:, at], low_ref[:, at]
        block = jnp.dot(top, high, preferred_element_type=F32)
        block += jnp.dot(top, low, preferred_element_type=F32) + jnp.dot(rest, high, preferred_element_type=F32)
        q_ref[pl.ds(cell, WIDTH, stride=CELLS), :] = block


def call(kernel, shapes, scratch=(), limit=32 << 20):
    spec = pl.BlockSpec(memory_space=pltpu.VMEM)
    return pl.pallas_call(
        kernel,
        out_shape=[jax.ShapeDtypeStruct(shape, dtype) for shape, dtype in shapes],
        out_specs=[spec] * len(shapes),
        scratch_shapes=list(scratch),
        compiler_params=pltpu.CompilerParams(vmem_limit_bytes=limit),
    )


def exchange(pieces, axes):
    return lax.all_to_all(pieces, axes, split_axis=0, concat_axis=0, tiled=True)


def summed_everywhere(packed):
    piece = exchange(packed, PLANE).sum(axis=0)
    piece = exchange(jnp.broadcast_to(piece, packed.shape), COLUMN).sum(axis=0)
    return exchange(jnp.broadcast_to(piece, packed.shape), PLANE)


def local(right_sides, coefficients):
    vectors = right_sides.reshape(VECTOR_ROWS, LANES)
    raw = coefficients.reshape(27 * CELLS, LANES)
    across, along = lax.axis_size(GX), lax.axis_size(GY)
    up = [(i, i + 1) for i in range(along - 1)]
    down = [(j, i) for i, j in up]
    near = [(i, i ^ 1) for i in range(across)]
    far = [(i, (i - 1) % across if i % 2 == 0 else (i + 1) % across) for i in range(across)]

    edge = ((EDGE_ROWS, LANES), F32)
    coefs, to_up, to_down = call(prepare_kernel, [((COEF_ROWS, LANES), F32), edge, edge])(vectors, raw)
    low = lax.ppermute(to_up, GY, up)
    high = lax.ppermute(to_down, GY, down)
    message = ((MESSAGE, LANES), F32)
    to_near, to_far = call(message_kernel, [message, message])(vectors, coefs, low, high)
    from_near = lax.ppermute(to_near, GX, near)
    from_far = lax.ppermute(to_far, GX, far)
    half = ((WIDTH, CELLS * LANES), BF16)
    top, rest, packed = call(
        basis_kernel,
        [half, half, ((32, LANES), F32)],
        [
            pltpu.VMEM((2, MESSAGE, LANES), F32),
            pltpu.VMEM((2, VECTOR_ROWS, LANES), F32),
            pltpu.VMEM((STEPS + 1, EXTENT, PLANES, 2, RHS, LANES), F32),
            pltpu.VMEM((2, EXTENT, PLANES, 2, RHS, LANES), F32),
            pltpu.VMEM((EXTENT - 2, 2, PER_ROW, LANES), F32),
            pltpu.VMEM((8, LANES), F32),
            pltpu.VMEM((WIDTH, LANES), F32),
        ],
    )(vectors, coefs, low, high, from_near, from_far)
    packed = summed_everywhere(packed)
    cells = CELLS * LANES * across * along
    q, r = call(
        functools.partial(finish_kernel, cells),
        [((WIDTH * CELLS, LANES), F32), ((WIDTH, WIDTH), F32)],
        [pltpu.VMEM((LANES, LANES), F32)],
    )(packed, top, rest)
    return q.reshape(WIDTH, PLANES, ROWS, LANES), r


def solution(mesh):
    mesh = Mesh(mesh.devices.reshape(4, 4, 2, 8, 4), ("y", "zh", "c", "zl", "x"))
    placed = P(None, None, GX, GY)
    return jax.shard_map(
        local,
        mesh=mesh,
        in_specs=(placed, placed),
        out_specs=(placed, P()),
        check_vma=False,
    )
```

```python
import functools

import jax
import jax.numpy as jnp
from jax import lax
from jax.experimental import pallas as pl
from jax.experimental.pallas import tpu as pltpu
from jax.sharding import Mesh, PartitionSpec as P

STEPS = 4
RHS = 16
WIDTH = RHS * (STEPS + 1)
ROWS = 4
PLANES = 4
LANES = 128
CELLS = ROWS * PLANES
REACH = STEPS

PLANE = ("y", "c", "x")
COLUMN = ("zh", "zl")
GX = ("y", "zh", "c")
GY = ("zl", "x")

FIRST_K = (0 + 9, 0, 0, 0)
LAST_K = (27, 27, 27, 18)
PLANE_AT = (0, 18, 45, 72)
PER_ROW = 96
VECTOR_ROWS = RHS * CELLS
COEF_ROWS = ROWS * PER_ROW
SENT_COEFS = (ROWS - 1) * PER_ROW
EDGE_ROWS = 24
MESSAGE = VECTOR_ROWS + SENT_COEFS + 2 * EDGE_ROWS
NEAR_ROWS = VECTOR_ROWS + SENT_COEFS - 6
VECTOR_GROUPS = VECTOR_ROWS // 8
COEF_GROUPS = COEF_ROWS // 8
EXTENT = ROWS + 2 * REACH

F32 = jnp.float32
BF16 = jnp.bfloat16


def lane_index(shape):
    return lax.broadcasted_iota(jnp.int32, shape, 1)


def spread(weights, x, end, row):
    return weights[x, end, pl.ds(row, 8, stride=0), :]


def prepare_kernel(v_ref, c_ref, coefs_ref, far_ref, near_ref):
    for x in range(ROWS):
        for z in range(PLANES):
            first, count = FIRST_K[z], LAST_K[z] - FIRST_K[z]
            rows = c_ref[pl.ds(first * CELLS + z * ROWS + x, count, stride=CELLS), :]
            number = first + lax.broadcasted_iota(jnp.int32, rows.shape, 0)
            rows = jnp.where(number == 13, 4.0 * rows - 6.0, 4.0 * rows)
            at = x * PER_ROW + PLANE_AT[z]
            coefs_ref[at : at + count, :] = rows
        at = x * PER_ROW + 90
        coefs_ref[at : at + 6, :] = jnp.zeros((6, LANES), F32)
    core = lax.axis_index("c")
    for ref, skip in ((near_ref, 1 - core), (far_ref, core)):
        start = pl.multiple_of(skip * PER_ROW, 8)
        ref[0:VECTOR_ROWS, :] = v_ref[...]
        count = ref.shape[0] - VECTOR_ROWS
        ref[VECTOR_ROWS:, :] = coefs_ref[pl.ds(start, SENT_COEFS), :][0:count]


def edge_kernel(v_ref, coefs_ref, up_ref, down_ref):
    slot = lane_index((8, LANES)) // 4
    zero = jnp.zeros((8, LANES), F32)
    up, down = [zero] * 3, [zero] * 3
    for group in range(VECTOR_GROUPS + COEF_GROUPS):
        if group < VECTOR_GROUPS:
            block = v_ref[8 * group : 8 * group + 8, :]
        else:
            at = 8 * (group - VECTOR_GROUPS)
            block = coefs_ref[at : at + 8, :]
        pack, place = divmod(group, 32)
        here = slot == place
        up[pack] = jnp.where(here, pltpu.roll(block, (4 * place + 4) % LANES, 1), up[pack])
        down[pack] = jnp.where(here, pltpu.roll(block, (4 * place) % LANES, 1), down[pack])
    for pack in range(3):
        up_ref[8 * pack : 8 * pack + 8, :] = up[pack]
        down_ref[8 * pack : 8 * pack + 8, :] = down[pack]


def corner_kernel(low_ref, high_ref, near_ref, far_ref):
    for ref in (near_ref, far_ref):
        ref[0:EDGE_ROWS, :] = low_ref[...]
        ref[EDGE_ROWS : 2 * EDGE_ROWS, :] = high_ref[...]
    far_ref[2 * EDGE_ROWS :, :] = jnp.zeros((8, LANES), F32)


def basis_kernel(
    v_ref, coefs_ref, low_ref, high_ref, near_ref, near_corner_ref, far_ref, far_corner_ref,
    split_ref, packed_ref,
    sides, flat, basis, shifted, weights, gram,
):
    core = lax.axis_index("c")
    lane = lane_index((8, LANES))
    wide = lane_index((RHS, LANES))
    at = VECTOR_ROWS + SENT_COEFS

    def place(near_side, far_side):
        sides[near_side, 0:NEAR_ROWS, :] = near_ref[...]
        sides[near_side, at:, :] = near_corner_ref[...]
        sides[far_side, 0:at, :] = far_ref[...]
        sides[far_side, at:, :] = far_corner_ref[0 : 2 * EDGE_ROWS, :]

    @pl.when(core == 0)
    def _():
        place(1, 0)

    @pl.when(core != 0)
    def _():
        place(0, 1)

    def both_ends(block, group, low, high):
        pack, place = divmod(group, 32)
        back = pltpu.roll(low[pack], (-(4 * place + 4)) % LANES, 1)
        left = jnp.where(lane >= LANES - 4, back, block)
        back = pltpu.roll(high[pack], (-(4 * place)) % LANES, 1)
        right = jnp.where(lane < 4, back, block)
        return left, right

    def put(step, x, z, end, value):
        basis[step, x, z, end] = value
        if step < STEPS:
            shifted[step % 2, 0, x, z, end] = pltpu.roll(value, 1, 1)
            shifted[step % 2, 1, x, z, end] = pltpu.roll(value, LANES - 1, 1)

    for tile in range(3):
        if tile == 1:
            vectors, coefs = v_ref, coefs_ref
            low = [low_ref[8 * p : 8 * p + 8, :] for p in range(3)]
            high = [high_ref[8 * p : 8 * p + 8, :] for p in range(3)]
            first_row, rows, skip = ROWS + REACH - ROWS, ROWS, 0
        else:
            side = sides.at[tile // 2]
            vectors, coefs = side, side.at[pl.ds(VECTOR_ROWS, SENT_COEFS)]
            low = [side[at + 8 * p : at + 8 * p + 8, :] for p in range(3)]
            high = [side[at + EDGE_ROWS + 8 * p : at + EDGE_ROWS + 8 * p + 8, :] for p in range(3)]
            first_row, rows = (0, ROWS - 1) if tile == 0 else (ROWS + REACH, ROWS - 1)
            skip = 1 if tile == 0 else 0
        for group in range(VECTOR_GROUPS):
            block = vectors[8 * group : 8 * group + 8, :]
            left, right = both_ends(block, group, low, high)
            flat[0, 8 * group : 8 * group + 8, :] = left
            flat[1, 8 * group : 8 * group + 8, :] = right
        for x in range(ROWS):
            for z in range(PLANES):
                for end in range(2):
                    value = flat[end, pl.ds(z * ROWS + x, RHS, stride=CELLS), :]
                    put(0, first_row + x, z, end, value)
        for x in range(rows):
            row = first_row + skip + x - 1
            for part in range(PER_ROW // 8):
                block = coefs[x * PER_ROW + 8 * part : x * PER_ROW + 8 * part + 8, :]
                group = VECTOR_GROUPS + (x + skip) * (PER_ROW // 8) + part
                left, right = both_ends(block, group, low, high)
                weights[row, 0, 8 * part : 8 * part + 8, :] = left
                weights[row, 1, 8 * part : 8 * part + 8, :] = right

    for step in range(1, STEPS + 1):
        first, last = step, EXTENT - step

        def one_row(x, _, step=step):
            for end in range(2):
                total = [None] * PLANES
                for dx in range(-1, 2):
                    for dy in range(-1, 2):
                        for source in range(PLANES):
                            if dy == 0:
                                value = basis[step - 1, x + dx, source, end]
                            else:
                                value = shifted[(step - 1) % 2, (dy + 1) // 2, x + dx, source, end]
                            for dz in range(-1, 2):
                                z = source - dz
                                if not 0 <= z < PLANES:
                                    continue
                                k = 9 * (dz + 1) + 3 * (dx + 1) + (dy + 1)
                                row = PLANE_AT[z] + k - FIRST_K[z]
                                weight = spread(weights, x - 1, end, row)
                                term = jnp.concatenate([weight, weight], axis=0) * value
                                total[z] = term if total[z] is None else total[z] + term
                for z in range(PLANES):
                    if step == 1:
                        total[z] = 0.5 * total[z]
                    else:
                        total[z] = total[z] - basis[step - 2, x, z, end]
                    put(step, x, z, end, total[z])
            return 0

        lax.fori_loop(first, last, one_row, 0)

    for step in range(STEPS + 1):
        for x in range(ROWS):
            for z in range(PLANES):
                left = basis[step, REACH + x, z, 0]
                right = basis[step, REACH + x, z, 1]
                value = jnp.where(wide < LANES // 2, left, right)
                rest = value - value.astype(BF16).astype(F32)
                cell = (z * ROWS + x) * LANES
                at = RHS * step
                split_ref[at : at + RHS, cell : cell + LANES] = value.astype(BF16)
                split_ref[2 * WIDTH + at : 2 * WIDTH + at + RHS, cell : cell + LANES] = value.astype(BF16)
                split_ref[WIDTH + at : WIDTH + at + RHS, cell : cell + LANES] = rest.astype(BF16)

    dims = (((1,), (1,)), ((), ()))
    both = split_ref[0 : 2 * WIDTH, :]
    products = lax.dot_general(both, both, dims, preferred_element_type=F32)
    crossed = products[0:WIDTH, WIDTH : 2 * WIDTH] + products[WIDTH : 2 * WIDTH, 0:WIDTH]
    gram[:, 0:WIDTH] = products[0:WIDTH, 0:WIDTH] + crossed
    lane32 = lane_index((32, LANES))
    packed = jnp.where(lane32 < WIDTH, gram[48:80, :], pltpu.roll(gram[16:48, :], WIDTH, 1))
    packed_ref[...] = packed
    packed_ref[0:16, :] = jnp.where(wide < 112, packed[0:16, :], pltpu.roll(gram[0:16, :], 112, 1))


def finish_kernel(cells, packed_ref, split_ref, q_ref, r_ref, square):
    packed = packed_ref[...] * (1.0 / cells)
    square[...] = jnp.zeros((LANES, LANES), F32)
    square[48:80, :] = packed
    square[16:48, :] = pltpu.roll(packed, 48, 1)
    square[0:16, :] = pltpu.roll(packed[0:16, :], 16, 1)
    whole = square[...]
    turned = whole.T
    row = lax.broadcasted_iota(jnp.int32, (LANES, LANES), 0)
    lane = lane_index((LANES, LANES))
    square[...] = jnp.where(lane <= row, whole, turned)
    lane = lane_index((8, LANES))
    inner = lax.broadcasted_iota(jnp.int32, (8, LANES), 0)
    groups = WIDTH // 8
    part = [square[8 * g : 8 * g + 8, :] for g in range(groups)]
    for own in range(groups):
        first = 8 * own
        inside = (lane >= first) & (lane < first + 8)
        rows = [jnp.broadcast_to(part[own][k : k + 1, :], (8, LANES)) for k in range(8)]
        small = {
            (k, l): jnp.broadcast_to(rows[k][:, first + l : first + l + 1], (8, LANES))
            for k in range(8)
            for l in range(k, 8)
        }
        rows = [jnp.where(inside, jnp.where(lane == first + k, 1.0, 0.0), rows[k]) for k in range(8)]
        over, factor = [None] * 8, {}
        for k in range(8):
            over[k] = 1.0 / small[k, k]
            for l in range(k + 1, 8):
                factor[l, k] = small[k, l] * over[k]
                for m in range(l, 8):
                    small[l, m] = small[l, m] - factor[l, k] * small[k, m]
                rows[l] = rows[l] - factor[l, k] * rows[k]
        solved = [None] * 8
        for k in reversed(range(8)):
            solved[k] = rows[k] * over[k]
            for l in range(k + 1, 8):
                solved[k] = solved[k] - factor[l, k] * solved[l]
        for g in range(own + 1, groups):
            total = jnp.where(inside, 0.0, part[g])
            for k in range(8):
                column = jnp.broadcast_to(part[g][:, first + k : first + k + 1], (8, LANES))
                total = total - column * solved[k]
            part[g] = total
        lower, upper = jnp.zeros((8, LANES), F32), jnp.zeros((8, LANES), F32)
        for k in range(8):
            scale = lax.rsqrt(small[k, k])
            lower = jnp.where(inner == k, rows[k] * scale, lower)
            high = rows[k]
            for l in range(k, 8):
                high = jnp.where(lane == first + l, small[k, l], high)
            upper = jnp.where(inner == k, high * scale, upper)
        r_ref[first : first + 8, :] = jnp.where(lane >= inner + first, upper, 0.0)[:, 0:WIDTH]
        square[first : first + 8, :] = jnp.where(lane <= inner + first, lower, 0.0)
    inverse = square[0:WIDTH, 0:WIDTH]
    top = inverse.astype(BF16)
    rest = (inverse - top.astype(F32)).astype(BF16)
    parts = jnp.concatenate([top, top, rest], axis=1)
    for cell in range(0, CELLS, 2):
        block = jnp.dot(parts, split_ref[:, cell * LANES : (cell + 2) * LANES], preferred_element_type=F32)
        q_ref[pl.ds(cell, WIDTH, stride=CELLS), :] = block[:, 0:LANES]
        q_ref[pl.ds(cell + 1, WIDTH, stride=CELLS), :] = block[:, LANES:]


def call(kernel, shapes, scratch=(), limit=32 << 20):
    spec = pl.BlockSpec(memory_space=pltpu.VMEM)
    return pl.pallas_call(
        kernel,
        out_shape=[jax.ShapeDtypeStruct(shape, dtype) for shape, dtype in shapes],
        out_specs=[spec] * len(shapes),
        scratch_shapes=list(scratch),
        compiler_params=pltpu.CompilerParams(vmem_limit_bytes=limit),
    )


def exchange(pieces, axes):
    return lax.all_to_all(pieces, axes, split_axis=0, concat_axis=0, tiled=True)


def summed_everywhere(packed):
    piece = exchange(packed, PLANE).sum(axis=0)
    piece = exchange(jnp.broadcast_to(piece, packed.shape), COLUMN).sum(axis=0)
    return exchange(jnp.broadcast_to(piece, packed.shape), PLANE)


def local(right_sides, coefficients):
    vectors = right_sides.reshape(VECTOR_ROWS, LANES)
    raw = coefficients.reshape(27 * CELLS, LANES)
    across, along = lax.axis_size(GX), lax.axis_size(GY)
    up = [(i, i + 1) for i in range(along - 1)]
    down = [(j, i) for i, j in up]
    near = [(i, i ^ 1) for i in range(across)]
    far = [(i, (i - 1) % across if i % 2 == 0 else (i + 1) % across) for i in range(across)]

    edge = ((EDGE_ROWS, LANES), F32)
    coefs, to_far, to_near = call(
        prepare_kernel,
        [((COEF_ROWS, LANES), F32), ((VECTOR_ROWS + SENT_COEFS, LANES), F32), ((NEAR_ROWS, LANES), F32)],
    )(vectors, raw)
    from_far = lax.ppermute(to_far, GX, far)
    from_near = lax.ppermute(to_near, GX, near)
    to_up, to_down = call(edge_kernel, [edge, edge])(vectors, coefs)
    low = lax.ppermute(to_up, GY, up)
    high = lax.ppermute(to_down, GY, down)
    sizes = [((2 * EDGE_ROWS + extra, LANES), F32) for extra in (0, 8)]
    to_near, to_far = call(corner_kernel, sizes)(low, high)
    far_corner = lax.ppermute(to_far, GX, far)
    near_corner = lax.ppermute(to_near, GX, near)
    split, packed = call(
        basis_kernel,
        [((3 * WIDTH, CELLS * LANES), BF16), ((32, LANES), F32)],
        [
            pltpu.VMEM((2, MESSAGE, LANES), F32),
            pltpu.VMEM((2, VECTOR_ROWS, LANES), F32),
            pltpu.VMEM((STEPS + 1, EXTENT, PLANES, 2, RHS, LANES), F32),
            pltpu.VMEM((2, 2, EXTENT, PLANES, 2, RHS, LANES), F32),
            pltpu.VMEM((EXTENT - 2, 2, PER_ROW, LANES), F32),
            pltpu.VMEM((WIDTH, LANES), F32),
        ],
    )(vectors, coefs, low, high, from_near, near_corner, from_far, far_corner)
    packed = summed_everywhere(packed)
    cells = CELLS * LANES * across * along
    q, r = call(
        functools.partial(finish_kernel, cells),
        [((WIDTH * CELLS, LANES), F32), ((WIDTH, WIDTH), F32)],
        [pltpu.VMEM((LANES, LANES), F32)],
    )(packed, split)
    return q.reshape(WIDTH, PLANES, ROWS, LANES), r


def solution(mesh):
    mesh = Mesh(mesh.devices.reshape(4, 4, 2, 8, 4), ("y", "zh", "c", "zl", "x"))
    placed = P(None, None, GX, GY)
    return jax.shard_map(
        local,
        mesh=mesh,
        in_specs=(placed, placed),
        out_specs=(placed, P()),
        check_vma=False,
    )
```

```python
import functools

import jax
import jax.numpy as jnp
from jax import lax
from jax.experimental import pallas as pl
from jax.experimental.pallas import tpu as pltpu
from jax.sharding import Mesh, PartitionSpec as P

STEPS = 4
RHS = 16
WIDTH = RHS * (STEPS + 1)
ROWS = 4
PLANES = 4
LANES = 128
CELLS = ROWS * PLANES
REACH = STEPS

PLANE = ("y", "c", "x")
COLUMN = ("zh", "zl")
GX = ("y", "zh", "c")
GY = ("zl", "x")

FIRST_K = (0 + 9, 0, 0, 0)
LAST_K = (27, 27, 27, 18)
PLANE_AT = (0, 18, 45, 72)
PER_ROW = 96
VECTOR_ROWS = RHS * CELLS
COEF_ROWS = ROWS * PER_ROW
USED = 90
SENT_COEFS = (ROWS - 1) * USED
EDGE_ROWS = 24
CORNER_ROWS = 16
NEAR_ROWS = VECTOR_ROWS + SENT_COEFS
FAR_ROWS = NEAR_ROWS + 2
SIDE_ROWS = NEAR_ROWS + 10
ROW_GROUPS = PER_ROW // 8
VECTOR_GROUPS = VECTOR_ROWS // 8
COEF_GROUPS = ROWS * ROW_GROUPS
EXTENT = ROWS + 2 * REACH

F32 = jnp.float32
BF16 = jnp.bfloat16


def lane_index(shape):
    return lax.broadcasted_iota(jnp.int32, shape, 1)


def spread(weights, x, end, row):
    return weights[x, end, pl.ds(row, 8, stride=0), :]


def prepare_kernel(v_ref, c_ref, coefs_ref, far_ref, near_ref, raw, sems):
    copies = [
        pltpu.make_async_copy(c_ref, raw, sems.at[0]),
        pltpu.make_async_copy(v_ref, far_ref.at[0:VECTOR_ROWS], sems.at[1]),
        pltpu.make_async_copy(v_ref, near_ref.at[0:VECTOR_ROWS], sems.at[2]),
    ]
    for copy in copies:
        copy.start()
    far_ref[NEAR_ROWS:, :] = jnp.zeros((FAR_ROWS - NEAR_ROWS, LANES), F32)
    copies[0].wait()
    for x in range(ROWS):
        for z in range(PLANES):
            first, count = FIRST_K[z], LAST_K[z] - FIRST_K[z]
            rows = raw[pl.ds(first * CELLS + z * ROWS + x, count, stride=CELLS), :]
            number = first + lax.broadcasted_iota(jnp.int32, rows.shape, 0)
            rows = jnp.where(number == 13, 4.0 * rows - 6.0, 4.0 * rows)
            at = x * PER_ROW + PLANE_AT[z]
            coefs_ref[at : at + count, :] = rows
        at = x * PER_ROW + USED
        coefs_ref[at : at + PER_ROW - USED, :] = jnp.zeros((PER_ROW - USED, LANES), F32)
    core = lax.axis_index("c")
    for ref, skip in ((near_ref, 1 - core), (far_ref, core)):
        for x in range(ROWS - 1):
            start = pl.multiple_of((skip + x) * PER_ROW, 8)
            at = VECTOR_ROWS + x * USED
            ref[at : at + USED, :] = coefs_ref[pl.ds(start, USED), :]
    copies[1].wait()
    copies[2].wait()


def edge_kernel(v_ref, coefs_ref, up_ref, down_ref):
    slot = lane_index((8, LANES)) // 4
    zero = jnp.zeros((8, LANES), F32)
    up, down = [zero] * 3, [zero] * 3
    for group in range(VECTOR_GROUPS + COEF_GROUPS):
        if group < VECTOR_GROUPS:
            block = v_ref[8 * group : 8 * group + 8, :]
        else:
            at = 8 * (group - VECTOR_GROUPS)
            block = coefs_ref[at : at + 8, :]
        pack, place = divmod(group, 32)
        here = slot == place
        up[pack] = jnp.where(here, pltpu.roll(block, (4 * place + 4) % LANES, 1), up[pack])
        down[pack] = jnp.where(here, pltpu.roll(block, (4 * place) % LANES, 1), down[pack])
    for pack in range(3):
        up_ref[8 * pack : 8 * pack + 8, :] = up[pack]
        down_ref[8 * pack : 8 * pack + 8, :] = down[pack]


def corner_kernel(low_ref, high_ref, near_ref, far_ref):
    core = lax.axis_index("c")
    lane = lane_index((8, LANES))
    for side, ref in enumerate((low_ref, high_ref)):
        at = CORNER_ROWS * side
        packs = [ref[8 * p : 8 * p + 8, :] for p in range(3)]
        made = []
        for skip in range(2):
            made.append(jnp.zeros((8, LANES), F32))
            for group in range((ROWS - 1) * ROW_GROUPS):
                pack, place = divmod(VECTOR_GROUPS + group + skip * ROW_GROUPS, 32)
                start = 4 * place + (1 if side == 0 else 0)
                moved = pltpu.roll(packs[pack], (3 * group - start) % LANES, 1)
                made[skip] = jnp.where((lane >= 3 * group) & (lane < 3 * group + 3), moved, made[skip])
        near_ref[at : at + 8, :] = packs[0]
        far_ref[at : at + 8, :] = packs[0]
        near_ref[at + 8 : at + 16, :] = jnp.where(core == 0, made[1], made[0])
        far_ref[at + 8 : at + 16, :] = jnp.where(core == 0, made[0], made[1])


def basis_kernel(
    far_ref, far_corner_ref, near_ref, near_corner_ref, own_ref, coefs_ref, low_ref, high_ref,
    split_ref, packed_ref,
    sides, corners, flat, basis, shifted, weights, gram,
):
    core = lax.axis_index("c")
    lane = lane_index((8, LANES))
    wide = lane_index((RHS, LANES))
    def place(near_side, far_side):
        sides[near_side, 0:NEAR_ROWS, :] = near_ref[...]
        sides[far_side, 0:NEAR_ROWS, :] = far_ref[0:NEAR_ROWS, :]
        corners[near_side] = near_corner_ref[...]
        corners[far_side] = far_corner_ref[...]

    @pl.when(core == 0)
    def _():
        place(1, 0)

    @pl.when(core != 0)
    def _():
        place(0, 1)

    def both_ends(block, low, high, place, width):
        offset = 4 - width
        back = pltpu.roll(low, (LANES - 4 + offset - width * place) % LANES, 1)
        left = jnp.where(lane >= LANES - width, back, block)
        back = pltpu.roll(high, (-width * place) % LANES, 1)
        right = jnp.where(lane < width, back, block)
        return left, right

    def put(step, x, z, end, value):
        basis[step, x, z, end] = value
        if step < STEPS:
            shifted[step % 2, 0, x, z, end] = pltpu.roll(value, 1, 1)
            shifted[step % 2, 1, x, z, end] = pltpu.roll(value, LANES - 1, 1)

    for tile in range(3):
        if tile == 1:
            vectors = own_ref
            low = [low_ref[8 * p : 8 * p + 8, :] for p in range(3)]
            high = [high_ref[8 * p : 8 * p + 8, :] for p in range(3)]
            first_row, rows, skip = REACH, ROWS, 0
        else:
            vectors, corner = sides.at[tile // 2], corners.at[tile // 2]
            low = [corner[8 * p : 8 * p + 8, :] for p in range(2)]
            high = [corner[CORNER_ROWS + 8 * p : CORNER_ROWS + 8 * p + 8, :] for p in range(2)]
            first_row, skip = (0, 1) if tile == 0 else (ROWS + REACH, 0)
            rows = ROWS - 1
        for group in range(VECTOR_GROUPS):
            block = vectors[8 * group : 8 * group + 8, :]
            left, right = both_ends(block, low[0], high[0], group, 4)
            flat[0, 8 * group : 8 * group + 8, :] = left
            flat[1, 8 * group : 8 * group + 8, :] = right
        for x in range(ROWS):
            for z in range(PLANES):
                for end in range(2):
                    value = flat[end, pl.ds(z * ROWS + x, RHS, stride=CELLS), :]
                    put(0, first_row + x, z, end, value)
        for x in range(rows):
            row = first_row + skip + x - 1
            for part in range(ROW_GROUPS):
                group = x * ROW_GROUPS + part
                if tile == 1:
                    block = coefs_ref[8 * group : 8 * group + 8, :]
                    pack, slot = divmod(VECTOR_GROUPS + group, 32)
                    left, right = both_ends(block, low[pack], high[pack], slot, 4)
                else:
                    at = VECTOR_ROWS + x * USED + 8 * part
                    block = vectors[at : at + 8, :]
                    left, right = both_ends(block, low[1], high[1], group, 3)
                weights[row, 0, 8 * part : 8 * part + 8, :] = left
                weights[row, 1, 8 * part : 8 * part + 8, :] = right

    for step in range(1, STEPS + 1):
        first, last = step, EXTENT - step

        def one_row(x, _, step=step):
            for end in range(2):
                total = [None] * PLANES
                for dx in range(-1, 2):
                    for dy in range(-1, 2):
                        for source in range(PLANES):
                            if dy == 0:
                                value = basis[step - 1, x + dx, source, end]
                            else:
                                value = shifted[(step - 1) % 2, (dy + 1) // 2, x + dx, source, end]
                            for dz in range(-1, 2):
                                z = source - dz
                                if not 0 <= z < PLANES:
                                    continue
                                k = 9 * (dz + 1) + 3 * (dx + 1) + (dy + 1)
                                row = PLANE_AT[z] + k - FIRST_K[z]
                                weight = spread(weights, x - 1, end, row)
                                term = jnp.concatenate([weight, weight], axis=0) * value
                                total[z] = term if total[z] is None else total[z] + term
                for z in range(PLANES):
                    if step == 1:
                        total[z] = 0.5 * total[z]
                    else:
                        total[z] = total[z] - basis[step - 2, x, z, end]
                    put(step, x, z, end, total[z])
            return 0

        lax.fori_loop(first, last, one_row, 0, unroll=True)

    for step in range(STEPS + 1):
        for x in range(ROWS):
            for z in range(PLANES):
                left = basis[step, REACH + x, z, 0]
                right = basis[step, REACH + x, z, 1]
                value = jnp.where(wide < LANES // 2, left, right)
                rest = value - value.astype(BF16).astype(F32)
                cell = (z * ROWS + x) * LANES
                at = RHS * step
                split_ref[at : at + RHS, cell : cell + LANES] = value.astype(BF16)
                split_ref[2 * WIDTH + at : 2 * WIDTH + at + RHS, cell : cell + LANES] = value.astype(BF16)
                split_ref[WIDTH + at : WIDTH + at + RHS, cell : cell + LANES] = rest.astype(BF16)

    dims = (((1,), (1,)), ((), ()))
    both = split_ref[0 : 2 * WIDTH, :]
    products = lax.dot_general(both, both, dims, preferred_element_type=F32)
    crossed = products[0:WIDTH, WIDTH : 2 * WIDTH] + products[WIDTH : 2 * WIDTH, 0:WIDTH]
    gram[:, 0:WIDTH] = products[0:WIDTH, 0:WIDTH] + crossed
    lane32 = lane_index((32, LANES))
    packed = jnp.where(lane32 < WIDTH, gram[48:80, :], pltpu.roll(gram[16:48, :], WIDTH, 1))
    packed_ref[...] = packed
    packed_ref[0:16, :] = jnp.where(wide < 112, packed[0:16, :], pltpu.roll(gram[0:16, :], 112, 1))


def finish_kernel(cells, packed_ref, split_ref, q_ref, r_ref, square):
    packed = packed_ref[...] * (1.0 / cells)
    square[...] = jnp.zeros((LANES, LANES), F32)
    square[48:80, :] = packed
    square[16:48, :] = pltpu.roll(packed, 48, 1)
    square[0:16, :] = pltpu.roll(packed[0:16, :], 16, 1)
    whole = square[...]
    turned = whole.T
    row = lax.broadcasted_iota(jnp.int32, (LANES, LANES), 0)
    lane = lane_index((LANES, LANES))
    square[...] = jnp.where(lane <= row, whole, turned)
    lane = lane_index((8, LANES))
    inner = lax.broadcasted_iota(jnp.int32, (8, LANES), 0)
    groups = WIDTH // 8
    part = [square[8 * g : 8 * g + 8, :] for g in range(groups)]
    for own in range(groups):
        first = 8 * own
        inside = (lane >= first) & (lane < first + 8)
        rows = [jnp.broadcast_to(part[own][k : k + 1, :], (8, LANES)) for k in range(8)]
        small = {
            (k, l): jnp.broadcast_to(rows[k][:, first + l : first + l + 1], (8, LANES))
            for k in range(8)
            for l in range(k, 8)
        }
        rows = [jnp.where(inside, jnp.where(lane == first + k, 1.0, 0.0), rows[k]) for k in range(8)]
        over, factor = [None] * 8, {}
        for k in range(8):
            over[k] = 1.0 / small[k, k]
            for l in range(k + 1, 8):
                factor[l, k] = small[k, l] * over[k]
                for m in range(l, 8):
                    small[l, m] = small[l, m] - factor[l, k] * small[k, m]
                rows[l] = rows[l] - factor[l, k] * rows[k]
        solved = [None] * 8
        for k in reversed(range(8)):
            solved[k] = rows[k] * over[k]
            for l in range(k + 1, 8):
                solved[k] = solved[k] - factor[l, k] * solved[l]
        for g in range(own + 1, groups):
            total = jnp.where(inside, 0.0, part[g])
            for k in range(8):
                column = jnp.broadcast_to(part[g][:, first + k : first + k + 1], (8, LANES))
                total = total - column * solved[k]
            part[g] = total
        lower, upper = jnp.zeros((8, LANES), F32), jnp.zeros((8, LANES), F32)
        for k in range(8):
            scale = lax.rsqrt(small[k, k])
            lower = jnp.where(inner == k, rows[k] * scale, lower)
            high = rows[k]
            for l in range(k, 8):
                high = jnp.where(lane == first + l, small[k, l], high)
            upper = jnp.where(inner == k, high * scale, upper)
        r_ref[first : first + 8, :] = jnp.where(lane >= inner + first, upper, 0.0)[:, 0:WIDTH]
        square[first : first + 8, :] = jnp.where(lane <= inner + first, lower, 0.0)
    inverse = square[0:WIDTH, 0:WIDTH]
    top = inverse.astype(BF16)
    rest = (inverse - top.astype(F32)).astype(BF16)
    parts = jnp.concatenate([top, top, rest], axis=1)
    for cell in range(0, CELLS, 2):
        block = jnp.dot(parts, split_ref[:, cell * LANES : (cell + 2) * LANES], preferred_element_type=F32)
        q_ref[pl.ds(cell, WIDTH, stride=CELLS), :] = block[:, 0:LANES]
        q_ref[pl.ds(cell + 1, WIDTH, stride=CELLS), :] = block[:, LANES:]


def call(kernel, inputs, shapes, scratch=(), space=pltpu.VMEM):
    return pl.pallas_call(
        kernel,
        out_shape=[jax.ShapeDtypeStruct(shape, dtype) for shape, dtype in shapes],
        in_specs=[pl.BlockSpec(memory_space=space)] * inputs,
        out_specs=[pl.BlockSpec(memory_space=pltpu.VMEM)] * len(shapes),
        scratch_shapes=list(scratch),
        compiler_params=pltpu.CompilerParams(vmem_limit_bytes=32 << 20),
    )


def exchange(pieces, axes):
    return lax.all_to_all(pieces, axes, split_axis=0, concat_axis=0, tiled=True)


def summed_everywhere(packed):
    piece = exchange(packed, PLANE).sum(axis=0)
    piece = exchange(jnp.broadcast_to(piece, packed.shape), COLUMN).sum(axis=0)
    return exchange(jnp.broadcast_to(piece, packed.shape), PLANE)


def local(right_sides, coefficients):
    vectors = right_sides.reshape(VECTOR_ROWS, LANES)
    raw = coefficients.reshape(27 * CELLS, LANES)
    across, along = lax.axis_size(GX), lax.axis_size(GY)
    up = [(i, i + 1) for i in range(along - 1)]
    down = [(j, i) for i, j in up]
    near = [(i, i ^ 1) for i in range(across)]
    far = [(i, (i - 1) % across if i % 2 == 0 else (i + 1) % across) for i in range(across)]

    edge = ((EDGE_ROWS, LANES), F32)
    coefs, to_far, to_near = call(
        prepare_kernel,
        2,
        [((COEF_ROWS, LANES), F32), ((FAR_ROWS, LANES), F32), ((NEAR_ROWS, LANES), F32)],
        [pltpu.VMEM((27 * CELLS, LANES), F32), pltpu.SemaphoreType.DMA((3,))],
        pltpu.HBM,
    )(*[pltpu.with_memory_space_constraint(t, pltpu.HBM) for t in (vectors, raw)])
    from_far = lax.ppermute(to_far, GX, far)
    from_near = lax.ppermute(to_near, GX, near)
    to_up, to_down = call(edge_kernel, 2, [edge, edge])(to_far, coefs)
    low = lax.ppermute(to_up, GY, up)
    high = lax.ppermute(to_down, GY, down)
    corner = ((2 * CORNER_ROWS, LANES), F32)
    near_corner, far_corner = call(corner_kernel, 2, [corner, corner])(low, high)
    far_corner = lax.ppermute(far_corner, GX, far)
    near_corner = lax.ppermute(near_corner, GX, near)
    split, packed = call(
        basis_kernel,
        8,
        [((3 * WIDTH, CELLS * LANES), BF16), ((32, LANES), F32)],
        [
            pltpu.VMEM((2, SIDE_ROWS, LANES), F32),
            pltpu.VMEM((2, 2 * CORNER_ROWS, LANES), F32),
            pltpu.VMEM((2, VECTOR_ROWS, LANES), F32),
            pltpu.VMEM((STEPS + 1, EXTENT, PLANES, 2, RHS, LANES), F32),
            pltpu.VMEM((2, 2, EXTENT, PLANES, 2, RHS, LANES), F32),
            pltpu.VMEM((EXTENT - 2, 2, PER_ROW, LANES), F32),
            pltpu.VMEM((WIDTH, LANES), F32),
        ],
    )(from_far, far_corner, from_near, near_corner, to_far, coefs, low, high)
    packed = summed_everywhere(packed)
    cells = CELLS * LANES * across * along
    q, r = call(
        functools.partial(finish_kernel, cells),
        2,
        [((WIDTH * CELLS, LANES), F32), ((WIDTH, WIDTH), F32)],
        [pltpu.VMEM((LANES, LANES), F32)],
    )(packed, split)
    return q.reshape(WIDTH, PLANES, ROWS, LANES), r


def solution(mesh):
    mesh = Mesh(mesh.devices.reshape(4, 4, 2, 8, 4), ("y", "zh", "c", "zl", "x"))
    placed = P(None, None, GX, GY)
    return jax.shard_map(
        local,
        mesh=mesh,
        in_specs=(placed, placed),
        out_specs=(placed, P()),
        check_vma=False,
    )
```

```python
import functools

import jax
import jax.numpy as jnp
from jax import lax
from jax.experimental import pallas as pl
from jax.experimental.pallas import tpu as pltpu
from jax.sharding import Mesh, PartitionSpec as P

STEPS = 4
RHS = 16
WIDTH = RHS * (STEPS + 1)
ROWS = 4
PLANES = 4
LANES = 128
CELLS = ROWS * PLANES
REACH = STEPS

PLANE = ("y", "c", "x")
COLUMN = ("zh", "zl")
GX = ("y", "zh", "c")
GY = ("zl", "x")

FIRST_K = (0 + 9, 0, 0, 0)
LAST_K = (27, 27, 27, 18)
PLANE_AT = (0, 18, 45, 72)
PER_ROW = 96
USED = 90
VECTOR_ROWS = RHS * CELLS
COEF_ROWS = ROWS * PER_ROW
SENT = 2
BLOCK_ROWS = SENT * PLANES * RHS
COEFS_AT = 2 * BLOCK_ROWS
NEAR_ROWS = COEFS_AT + SENT * USED
FAR_ROWS = NEAR_ROWS + 2
SIDE_ROWS = NEAR_ROWS + 12
EDGE_ROWS = 24
CORNER_ROWS = 16
ROW_GROUPS = PER_ROW // 8
VECTOR_GROUPS = VECTOR_ROWS // 8
COEF_GROUPS = ROWS * ROW_GROUPS
BLOCK_GROUPS = BLOCK_ROWS // 8
EXTENT = ROWS + 2 * REACH

F32 = jnp.float32
BF16 = jnp.bfloat16


def lane_index(shape):
    return lax.broadcasted_iota(jnp.int32, shape, 1)


def spread(ref, at, row):
    return ref[(*at, pl.ds(row, 8, stride=0), slice(None))]


def stencil(get, weight):
    total = [None] * PLANES
    for dx in range(-1, 2):
        for dy in range(-1, 2):
            for source in range(PLANES):
                value = get(dx, dy, source)
                for dz in range(-1, 2):
                    z = source - dz
                    if not 0 <= z < PLANES:
                        continue
                    k = 9 * (dz + 1) + 3 * (dx + 1) + (dy + 1)
                    factor = weight(PLANE_AT[z] + k - FIRST_K[z])
                    term = jnp.concatenate([factor, factor], axis=0) * value
                    total[z] = term if total[z] is None else total[z] + term
    return total


def three(value):
    return (pltpu.roll(value, 1, 1), value, pltpu.roll(value, LANES - 1, 1))


def prepare_kernel(v_ref, c_ref, coefs_ref, own_ref, far_ref, near_ref, raw, turned, sems):
    copies = [
        pltpu.make_async_copy(v_ref, own_ref, sems.at[0]),
        pltpu.make_async_copy(c_ref, raw, sems.at[1]),
    ]
    for copy in copies:
        copy.start()
    far_ref[NEAR_ROWS:, :] = jnp.zeros((FAR_ROWS - NEAR_ROWS, LANES), F32)
    core = lax.axis_index("c")
    copies[0].wait()
    for x in range(ROWS):
        for z in range(PLANES):
            value = own_ref[pl.ds(z * ROWS + x, RHS, stride=CELLS), :]
            for shift, moved in enumerate(three(value)):
                turned[shift, x, z] = moved
    copies[1].wait()
    for x in range(ROWS):
        for z in range(PLANES):
            first, count = FIRST_K[z], LAST_K[z] - FIRST_K[z]
            rows = raw[pl.ds(first * CELLS + z * ROWS + x, count, stride=CELLS), :]
            number = first + lax.broadcasted_iota(jnp.int32, rows.shape, 0)
            rows = jnp.where(number == 13, 4.0 * rows - 6.0, 4.0 * rows)
            at = x * PER_ROW + PLANE_AT[z]
            coefs_ref[at : at + count, :] = rows
        at = x * PER_ROW + USED
        coefs_ref[at : at + PER_ROW - USED, :] = jnp.zeros((PER_ROW - USED, LANES), F32)
    for ref, last in ((near_ref, core == 0), (far_ref, core != 0)):
        skip = jnp.where(last, 2, 0)
        for x in range(SENT):
            for z in range(PLANES):
                at = (x * PLANES + z) * RHS
                ref[at : at + RHS, :] = turned[1, skip + x, z]
            start = pl.multiple_of((skip + x) * PER_ROW, 8)
            at = COEFS_AT + x * USED
            ref[at : at + USED, :] = coefs_ref[pl.ds(start, USED), :]
    for x in range(SENT):
        row = 1 + x
        total = stencil(
            lambda dx, dy, z: turned[dy + 1, row + dx, z],
            lambda k: spread(coefs_ref, (), row * PER_ROW + k),
        )
        for z in range(PLANES):
            at = BLOCK_ROWS + (x * PLANES + z) * RHS
            value = 0.5 * total[z]
            near_ref[at : at + RHS, :] = value
            far_ref[at : at + RHS, :] = value


def edge_kernel(v_ref, coefs_ref, up_ref, down_ref):
    slot = lane_index((8, LANES)) // 4
    zero = jnp.zeros((8, LANES), F32)
    up, down = [zero] * 3, [zero] * 3
    for group in range(VECTOR_GROUPS + COEF_GROUPS):
        if group < VECTOR_GROUPS:
            block = v_ref[8 * group : 8 * group + 8, :]
        else:
            at = 8 * (group - VECTOR_GROUPS)
            block = coefs_ref[at : at + 8, :]
        pack, place = divmod(group, 32)
        here = slot == place
        up[pack] = jnp.where(here, pltpu.roll(block, (4 * place + 4) % LANES, 1), up[pack])
        down[pack] = jnp.where(here, pltpu.roll(block, (4 * place) % LANES, 1), down[pack])
    for pack in range(3):
        up_ref[8 * pack : 8 * pack + 8, :] = up[pack]
        down_ref[8 * pack : 8 * pack + 8, :] = down[pack]


def patched(block, pack, slot, width, start, mask):
    return jnp.where(mask, pltpu.roll(pack, (start - width * slot) % LANES, 1), block)


def packs_of(ref, at, count):
    return [ref[at + 8 * p : at + 8 * p + 8, :] for p in range(count)]


def own_kernel(
    own_ref, coefs_ref, low_ref, high_ref,
    near_ref, far_ref, start_ref, first_ref, weights_ref,
    flat, fresh,
):
    core = lax.axis_index("c")
    lane = lane_index((8, LANES))
    low, high = packs_of(low_ref, 0, 3), packs_of(high_ref, 0, 3)
    for group in range(VECTOR_GROUPS + COEF_GROUPS):
        pack, slot = divmod(group, 32)
        if group < VECTOR_GROUPS:
            block = own_ref[8 * group : 8 * group + 8, :]
        else:
            at = 8 * (group - VECTOR_GROUPS)
            block = coefs_ref[at : at + 8, :]
        ends = (
            patched(block, low[pack], slot, 4, LANES - 4, lane >= LANES - 4),
            patched(block, high[pack], slot, 4, 0, lane < 4),
        )
        for end in range(2):
            if group < VECTOR_GROUPS:
                flat[end, 8 * group : 8 * group + 8, :] = ends[end]
            else:
                x, part = divmod(group - VECTOR_GROUPS, ROW_GROUPS)
                weights_ref[x, end, 8 * part : 8 * part + 8, :] = ends[end]
    for x in range(ROWS):
        for z in range(PLANES):
            for end in range(2):
                value = flat[end, pl.ds(z * ROWS + x, RHS, stride=CELLS), :]
                for shift, moved in enumerate(three(value)):
                    start_ref[shift, x, z, end] = moved
    for x in range(SENT):
        for end in range(2):
            row = 1 + x
            total = stencil(
                lambda dx, dy, z: start_ref[dy + 1, row + dx, z, end],
                lambda k: spread(weights_ref, (row, end), k),
            )
            for z in range(PLANES):
                for shift, moved in enumerate(three(0.5 * total[z])):
                    first_ref[shift, x, z, end] = moved
                    if shift == 1:
                        at = (x * PLANES + z) * RHS
                        fresh[end, at : at + RHS, :] = moved
    slot4 = lane // 4
    for end in range(2):
        common = jnp.zeros((8, LANES), F32)
        origin = LANES - 3 if end == 0 else LANES - 1
        for group in range(BLOCK_GROUPS):
            block = fresh[end, 8 * group : 8 * group + 8, :]
            slot = BLOCK_GROUPS + group
            common = jnp.where(slot4 == slot, pltpu.roll(block, (4 * slot - origin) % LANES, 1), common)
        blocks, coefs = [], []
        for skip in (0, 2):
            pack = common
            origin = LANES - 4 if end == 0 else 0
            for group in range(BLOCK_GROUPS):
                x, rest = divmod(group, 2 * PLANES)
                z, half = divmod(rest, 2)
                block = start_ref[1, skip + x, z, end, 8 * half : 8 * half + 8, :]
                pack = jnp.where(slot4 == group, pltpu.roll(block, (4 * group - origin) % LANES, 1), pack)
            blocks.append(pack)
            pack = jnp.zeros((8, LANES), F32)
            origin = LANES - 3 if end == 0 else 0
            for group in range(SENT * ROW_GROUPS):
                x, part = divmod(group, ROW_GROUPS)
                block = weights_ref[skip + x, end, 8 * part : 8 * part + 8, :]
                here = (lane >= 3 * group) & (lane < 3 * group + 3)
                pack = jnp.where(here, pltpu.roll(block, (3 * group - origin) % LANES, 1), pack)
            coefs.append(pack)
        at = CORNER_ROWS * end
        near_ref[at : at + 8, :] = jnp.where(core == 0, blocks[1], blocks[0])
        far_ref[at : at + 8, :] = jnp.where(core == 0, blocks[0], blocks[1])
        near_ref[at + 8 : at + 16, :] = jnp.where(core == 0, coefs[1], coefs[0])
        far_ref[at + 8 : at + 16, :] = jnp.where(core == 0, coefs[0], coefs[1])


def basis_kernel(
    far_ref, far_corner_ref, near_ref, near_corner_ref, start_ref, first_ref, own_weights_ref,
    split_ref, packed_ref,
    sides, corners, basis, side_weights, gram,
):
    core = lax.axis_index("c")
    lane = lane_index((8, LANES))
    wide = lane_index((RHS, LANES))

    def place(near_side, far_side):
        sides[near_side, 0:NEAR_ROWS, :] = near_ref[...]
        sides[far_side, 0:NEAR_ROWS, :] = far_ref[0:NEAR_ROWS, :]
        corners[near_side] = near_corner_ref[...]
        corners[far_side] = far_corner_ref[...]

    @pl.when(core == 0)
    def _():
        place(1, 0)

    @pl.when(core != 0)
    def _():
        place(0, 1)

    def put(step, x, z, end, value):
        if step == STEPS:
            basis[step, 1, x, z, end] = value
            return
        for shift, moved in enumerate(three(value)):
            basis[step, shift, x, z, end] = moved

    def get(step, dy, x, z, end):
        own = x - REACH
        if step == 0 and 0 <= own < ROWS:
            return start_ref[dy + 1, own, z, end]
        if step == 1 and 1 <= own <= 2:
            return first_ref[dy + 1, own - 1, z, end]
        return basis[step, dy + 1, x, z, end]

    def weight(x, end, k):
        own = x - REACH
        if 0 <= own < ROWS:
            return spread(own_weights_ref, (own, end), k)
        side, row = (0, x - 2) if own < 0 else (1, x - REACH - ROWS)
        return spread(side_weights, (side, row, end), k)

    for side in range(2):
        low = packs_of(corners.at[side], 0, 2)
        high = packs_of(corners.at[side], CORNER_ROWS, 2)
        for step in range(2):
            if step == 0:
                places = (LANES - 4, lane >= LANES - 4), (0, lane < 4)
                first = 2 if side == 0 else REACH + ROWS
            else:
                places = (LANES - 3, (lane >= LANES - 3) | (lane == 0)), (LANES - 1, (lane < 3) | (lane == LANES - 1))
                first = 1 if side == 0 else REACH + ROWS + 1
            for x in range(SENT):
                for z in range(PLANES):
                    for half in range(2):
                        slot = step * BLOCK_GROUPS + (x * PLANES + z) * 2 + half
                        block = sides[side, 8 * slot : 8 * slot + 8, :]
                        for end, pack in enumerate((low[0], high[0])):
                            value = patched(block, pack, slot, 4, *places[end])
                            basis[step, 1, first + x, z, end, 8 * half : 8 * half + 8, :] = value
        for x in range(SENT):
            for part in range(ROW_GROUPS):
                slot = x * ROW_GROUPS + part
                at = COEFS_AT + x * USED + 8 * part
                block = sides[side, at : at + 8, :]
                at = slice(8 * part, 8 * part + 8)
                side_weights[side, x, 0, at, :] = patched(block, low[1], slot, 3, LANES - 3, lane >= LANES - 3)
                side_weights[side, x, 1, at, :] = patched(block, high[1], slot, 3, 0, lane < 3)

    for step, rows in ((0, (2, 3, 8, 9)), (1, (1, 2, 9, 10))):
        for x in rows:
            for z in range(PLANES):
                for end in range(2):
                    value = basis[step, 1, x, z, end]
                    basis[step, 0, x, z, end] = pltpu.roll(value, 1, 1)
                    basis[step, 2, x, z, end] = pltpu.roll(value, LANES - 1, 1)

    for step in range(1, STEPS + 1):
        rows = range(step, EXTENT - step) if step > 1 else (3, 4, 7, 8)
        for x in rows:
            for end in range(2):
                total = stencil(
                    lambda dx, dy, z: get(step - 1, dy, x + dx, z, end),
                    lambda k: weight(x, end, k),
                )
                for z in range(PLANES):
                    value = 0.5 * total[z] if step == 1 else total[z] - get(step - 2, 0, x, z, end)
                    put(step, x, z, end, value)

    for step in range(STEPS + 1):
        for x in range(ROWS):
            for z in range(PLANES):
                left, right = (get(step, 0, REACH + x, z, end) for end in range(2))
                value = jnp.where(wide < LANES // 2, left, right)
                rest = value - value.astype(BF16).astype(F32)
                cell = (z * ROWS + x) * LANES
                at = RHS * step
                split_ref[at : at + RHS, cell : cell + LANES] = value.astype(BF16)
                split_ref[2 * WIDTH + at : 2 * WIDTH + at + RHS, cell : cell + LANES] = value.astype(BF16)
                split_ref[WIDTH + at : WIDTH + at + RHS, cell : cell + LANES] = rest.astype(BF16)

    dims = (((1,), (1,)), ((), ()))
    both = split_ref[0 : 2 * WIDTH, :]
    products = lax.dot_general(both, both, dims, preferred_element_type=F32)
    crossed = products[0:WIDTH, WIDTH : 2 * WIDTH] + products[WIDTH : 2 * WIDTH, 0:WIDTH]
    gram[:, 0:WIDTH] = products[0:WIDTH, 0:WIDTH] + crossed
    lane32 = lane_index((32, LANES))
    packed = jnp.where(lane32 < WIDTH, gram[48:80, :], pltpu.roll(gram[16:48, :], WIDTH, 1))
    packed_ref[...] = packed
    packed_ref[0:16, :] = jnp.where(wide < 112, packed[0:16, :], pltpu.roll(gram[0:16, :], 112, 1))


def finish_kernel(cells, packed_ref, split_ref, q_ref, r_ref, square):
    packed = packed_ref[...] * (1.0 / cells)
    square[...] = jnp.zeros((LANES, LANES), F32)
    square[48:80, :] = packed
    square[16:48, :] = pltpu.roll(packed, 48, 1)
    square[0:16, :] = pltpu.roll(packed[0:16, :], 16, 1)
    whole = square[...]
    turned = whole.T
    row = lax.broadcasted_iota(jnp.int32, (LANES, LANES), 0)
    lane = lane_index((LANES, LANES))
    square[...] = jnp.where(lane <= row, whole, turned)
    lane = lane_index((8, LANES))
    inner = lax.broadcasted_iota(jnp.int32, (8, LANES), 0)
    groups = WIDTH // 8
    part = [square[8 * g : 8 * g + 8, :] for g in range(groups)]
    for own in range(groups):
        first = 8 * own
        inside = (lane >= first) & (lane < first + 8)
        rows = [jnp.broadcast_to(part[own][k : k + 1, :], (8, LANES)) for k in range(8)]
        small = {
            (k, l): jnp.broadcast_to(rows[k][:, first + l : first + l + 1], (8, LANES))
            for k in range(8)
            for l in range(k, 8)
        }
        rows = [jnp.where(inside, jnp.where(lane == first + k, 1.0, 0.0), rows[k]) for k in range(8)]
        over, factor = [None] * 8, {}
        for k in range(8):
            over[k] = 1.0 / small[k, k]
            for l in range(k + 1, 8):
                factor[l, k] = small[k, l] * over[k]
                for m in range(l, 8):
                    small[l, m] = small[l, m] - factor[l, k] * small[k, m]
                rows[l] = rows[l] - factor[l, k] * rows[k]
        solved = [None] * 8
        for k in reversed(range(8)):
            solved[k] = rows[k] * over[k]
            for l in range(k + 1, 8):
                solved[k] = solved[k] - factor[l, k] * solved[l]
        for g in range(own + 1, groups):
            total = jnp.where(inside, 0.0, part[g])
            for k in range(8):
                column = jnp.broadcast_to(part[g][:, first + k : first + k + 1], (8, LANES))
                total = total - column * solved[k]
            part[g] = total
        lower, upper = jnp.zeros((8, LANES), F32), jnp.zeros((8, LANES), F32)
        for k in range(8):
            scale = lax.rsqrt(small[k, k])
            lower = jnp.where(inner == k, rows[k] * scale, lower)
            high = rows[k]
            for l in range(k, 8):
                high = jnp.where(lane == first + l, small[k, l], high)
            upper = jnp.where(inner == k, high * scale, upper)
        r_ref[first : first + 8, :] = jnp.where(lane >= inner + first, upper, 0.0)[:, 0:WIDTH]
        square[first : first + 8, :] = jnp.where(lane <= inner + first, lower, 0.0)
    inverse = square[0:WIDTH, 0:WIDTH]
    top = inverse.astype(BF16)
    rest = (inverse - top.astype(F32)).astype(BF16)
    parts = jnp.concatenate([top, top, rest], axis=1)
    for cell in range(0, CELLS, 2):
        block = jnp.dot(parts, split_ref[:, cell * LANES : (cell + 2) * LANES], preferred_element_type=F32)
        q_ref[pl.ds(cell, WIDTH, stride=CELLS), :] = block[:, 0:LANES]
        q_ref[pl.ds(cell + 1, WIDTH, stride=CELLS), :] = block[:, LANES:]


def call(kernel, inputs, shapes, scratch=(), space=pltpu.VMEM):
    return pl.pallas_call(
        kernel,
        out_shape=[jax.ShapeDtypeStruct(shape, dtype) for shape, dtype in shapes],
        in_specs=[pl.BlockSpec(memory_space=space)] * inputs,
        out_specs=[pl.BlockSpec(memory_space=pltpu.VMEM)] * len(shapes),
        scratch_shapes=list(scratch),
        compiler_params=pltpu.CompilerParams(vmem_limit_bytes=32 << 20),
    )


def exchange(pieces, axes):
    return lax.all_to_all(pieces, axes, split_axis=0, concat_axis=0, tiled=True)


def summed_everywhere(packed):
    piece = exchange(packed, PLANE).sum(axis=0)
    piece = exchange(jnp.broadcast_to(piece, packed.shape), COLUMN).sum(axis=0)
    return exchange(jnp.broadcast_to(piece, packed.shape), PLANE)


def local(right_sides, coefficients):
    vectors = right_sides.reshape(VECTOR_ROWS, LANES)
    raw = coefficients.reshape(27 * CELLS, LANES)
    across, along = lax.axis_size(GX), lax.axis_size(GY)
    up = [(i, i + 1) for i in range(along - 1)]
    down = [(j, i) for i, j in up]
    near = [(i, i ^ 1) for i in range(across)]
    far = [(i, (i - 1) % across if i % 2 == 0 else (i + 1) % across) for i in range(across)]

    edge = ((EDGE_ROWS, LANES), F32)
    coefs, own, to_far, to_near = call(
        prepare_kernel,
        2,
        [((rows, LANES), F32) for rows in (COEF_ROWS, VECTOR_ROWS, FAR_ROWS, NEAR_ROWS)],
        [
            pltpu.VMEM((27 * CELLS, LANES), F32),
            pltpu.VMEM((3, ROWS, PLANES, RHS, LANES), F32),
            pltpu.SemaphoreType.DMA((2,)),
        ],
        pltpu.HBM,
    )(*[pltpu.with_memory_space_constraint(t, pltpu.HBM) for t in (vectors, raw)])
    from_far = lax.ppermute(to_far, GX, far)
    from_near = lax.ppermute(to_near, GX, near)
    to_up, to_down = call(edge_kernel, 2, [edge, edge])(own, coefs)
    low = lax.ppermute(to_up, GY, up)
    high = lax.ppermute(to_down, GY, down)
    corner = ((2 * CORNER_ROWS, LANES), F32)
    near_corner, far_corner, start, first, weights = call(
        own_kernel,
        4,
        [
            corner,
            corner,
            ((3, ROWS, PLANES, 2, RHS, LANES), F32),
            ((3, SENT, PLANES, 2, RHS, LANES), F32),
            ((ROWS, 2, PER_ROW, LANES), F32),
        ],
        [pltpu.VMEM((2, VECTOR_ROWS, LANES), F32), pltpu.VMEM((2, BLOCK_ROWS, LANES), F32)],
    )(own, coefs, low, high)
    far_corner = lax.ppermute(far_corner, GX, far)
    near_corner = lax.ppermute(near_corner, GX, near)
    split, packed = call(
        basis_kernel,
        7,
        [((3 * WIDTH, CELLS * LANES), BF16), ((32, LANES), F32)],
        [
            pltpu.VMEM((2, SIDE_ROWS, LANES), F32),
            pltpu.VMEM((2, 2 * CORNER_ROWS, LANES), F32),
            pltpu.VMEM((STEPS + 1, 3, EXTENT, PLANES, 2, RHS, LANES), F32),
            pltpu.VMEM((2, SENT, 2, PER_ROW, LANES), F32),
            pltpu.VMEM((WIDTH, LANES), F32),
        ],
    )(from_far, far_corner, from_near, near_corner, start, first, weights)
    packed = summed_everywhere(packed)
    cells = CELLS * LANES * across * along
    q, r = call(
        functools.partial(finish_kernel, cells),
        2,
        [((WIDTH * CELLS, LANES), F32), ((WIDTH, WIDTH), F32)],
        [pltpu.VMEM((LANES, LANES), F32)],
    )(packed, split)
    return q.reshape(WIDTH, PLANES, ROWS, LANES), r


def solution(mesh):
    mesh = Mesh(mesh.devices.reshape(4, 4, 2, 8, 4), ("y", "zh", "c", "zl", "x"))
    placed = P(None, None, GX, GY)
    return jax.shard_map(
        local,
        mesh=mesh,
        in_specs=(placed, placed),
        out_specs=(placed, P()),
        check_vma=False,
    )
```

```python
import functools

import jax
import jax.numpy as jnp
from jax import lax
from jax.experimental import pallas as pl
from jax.experimental.pallas import tpu as pltpu
from jax.sharding import Mesh, PartitionSpec as P

STEPS = 4
RHS = 16
WIDTH = RHS * (STEPS + 1)
ROWS = 4
PLANES = 4
LANES = 128
CELLS = ROWS * PLANES
REACH = STEPS

PLANE = ("y", "c", "x")
COLUMN = ("zh", "zl")
GX = ("y", "zh", "c")
GY = ("zl", "x")

FIRST_K = (0 + 9, 0, 0, 0)
LAST_K = (27, 27, 27, 18)
PLANE_AT = (0, 18, 45, 72)
PER_ROW = 96
USED = 90
VECTOR_ROWS = RHS * CELLS
COEF_ROWS = ROWS * PER_ROW
SENT = 2
BLOCK_ROWS = SENT * PLANES * RHS
COEFS_AT = 2 * BLOCK_ROWS
NEAR_ROWS = COEFS_AT + SENT * USED
FAR_ROWS = NEAR_ROWS + 2
SIDE_ROWS = NEAR_ROWS + 12
EDGE_ROWS = 24
CORNER_ROWS = 16
ROW_GROUPS = PER_ROW // 8
VECTOR_GROUPS = VECTOR_ROWS // 8
COEF_GROUPS = ROWS * ROW_GROUPS
BLOCK_GROUPS = BLOCK_ROWS // 8
EXTENT = ROWS + 2 * REACH

F32 = jnp.float32
BF16 = jnp.bfloat16


def lane_index(shape):
    return lax.broadcasted_iota(jnp.int32, shape, 1)


def spread(ref, at, row):
    return ref[(*at, pl.ds(row, 8, stride=0), slice(None))]


def stencil(get, weight):
    total = [None] * PLANES
    for dx in range(-1, 2):
        for dy in range(-1, 2):
            for source in range(PLANES):
                value = get(dx, dy, source)
                for dz in range(-1, 2):
                    z = source - dz
                    if not 0 <= z < PLANES:
                        continue
                    k = 9 * (dz + 1) + 3 * (dx + 1) + (dy + 1)
                    factor = weight(PLANE_AT[z] + k - FIRST_K[z])
                    term = jnp.concatenate([factor, factor], axis=0) * value
                    total[z] = term if total[z] is None else total[z] + term
    return total


def three(value):
    return (pltpu.roll(value, 1, 1), value, pltpu.roll(value, LANES - 1, 1))


def prepare_kernel(v_ref, c_ref, coefs_ref, own_ref, far_ref, near_ref, raw, turned, sems):
    copies = [
        pltpu.make_async_copy(v_ref, own_ref, sems.at[0]),
        pltpu.make_async_copy(c_ref, raw, sems.at[1]),
    ]
    for copy in copies:
        copy.start()
    far_ref[NEAR_ROWS:, :] = jnp.zeros((FAR_ROWS - NEAR_ROWS, LANES), F32)
    core = lax.axis_index("c")
    copies[0].wait()
    for x in range(ROWS):
        for z in range(PLANES):
            value = own_ref[pl.ds(z * ROWS + x, RHS, stride=CELLS), :]
            for shift, moved in enumerate(three(value)):
                turned[shift, x, z] = moved
    copies[1].wait()
    for x in range(ROWS):
        for z in range(PLANES):
            first, count = FIRST_K[z], LAST_K[z] - FIRST_K[z]
            rows = raw[pl.ds(first * CELLS + z * ROWS + x, count, stride=CELLS), :]
            number = first + lax.broadcasted_iota(jnp.int32, rows.shape, 0)
            rows = jnp.where(number == 13, 4.0 * rows - 6.0, 4.0 * rows)
            at = x * PER_ROW + PLANE_AT[z]
            coefs_ref[at : at + count, :] = rows
        at = x * PER_ROW + USED
        coefs_ref[at : at + PER_ROW - USED, :] = jnp.zeros((PER_ROW - USED, LANES), F32)
    for ref, last in ((near_ref, core == 0), (far_ref, core != 0)):
        skip = jnp.where(last, 2, 0)
        for x in range(SENT):
            for z in range(PLANES):
                at = (x * PLANES + z) * RHS
                ref[at : at + RHS, :] = turned[1, skip + x, z]
            start = pl.multiple_of((skip + x) * PER_ROW, 8)
            at = COEFS_AT + x * USED
            ref[at : at + USED, :] = coefs_ref[pl.ds(start, USED), :]
    for x in range(SENT):
        row = 1 + x
        total = stencil(
            lambda dx, dy, z: turned[dy + 1, row + dx, z],
            lambda k: spread(coefs_ref, (), row * PER_ROW + k),
        )
        for z in range(PLANES):
            at = BLOCK_ROWS + (x * PLANES + z) * RHS
            value = 0.5 * total[z]
            near_ref[at : at + RHS, :] = value
            far_ref[at : at + RHS, :] = value


def edge_kernel(v_ref, coefs_ref, up_ref, down_ref):
    slot = lane_index((8, LANES)) // 4
    zero = jnp.zeros((8, LANES), F32)
    up, down = [zero] * 3, [zero] * 3
    for group in range(VECTOR_GROUPS + COEF_GROUPS):
        if group < VECTOR_GROUPS:
            block = v_ref[8 * group : 8 * group + 8, :]
        else:
            at = 8 * (group - VECTOR_GROUPS)
            block = coefs_ref[at : at + 8, :]
        pack, place = divmod(group, 32)
        here = slot == place
        up[pack] = jnp.where(here, pltpu.roll(block, (4 * place + 4) % LANES, 1), up[pack])
        down[pack] = jnp.where(here, pltpu.roll(block, (4 * place) % LANES, 1), down[pack])
    for pack in range(3):
        up_ref[8 * pack : 8 * pack + 8, :] = up[pack]
        down_ref[8 * pack : 8 * pack + 8, :] = down[pack]


def patched(block, pack, slot, width, start, mask):
    return jnp.where(mask, pltpu.roll(pack, (start - width * slot) % LANES, 1), block)


def packs_of(ref, at, count):
    return [ref[at + 8 * p : at + 8 * p + 8, :] for p in range(count)]


def own_kernel(
    own_ref, coefs_ref, low_ref, high_ref,
    near_ref, far_ref, start_ref, first_ref, weights_ref,
    flat, fresh,
):
    core = lax.axis_index("c")
    lane = lane_index((8, LANES))
    low, high = packs_of(low_ref, 0, 3), packs_of(high_ref, 0, 3)
    for group in range(VECTOR_GROUPS + COEF_GROUPS):
        pack, slot = divmod(group, 32)
        if group < VECTOR_GROUPS:
            block = own_ref[8 * group : 8 * group + 8, :]
        else:
            at = 8 * (group - VECTOR_GROUPS)
            block = coefs_ref[at : at + 8, :]
        ends = (
            patched(block, low[pack], slot, 4, LANES - 4, lane >= LANES - 4),
            patched(block, high[pack], slot, 4, 0, lane < 4),
        )
        for end in range(2):
            if group < VECTOR_GROUPS:
                flat[end, 8 * group : 8 * group + 8, :] = ends[end]
            else:
                x, part = divmod(group - VECTOR_GROUPS, ROW_GROUPS)
                weights_ref[x, end, 8 * part : 8 * part + 8, :] = ends[end]
    for x in range(ROWS):
        for z in range(PLANES):
            for end in range(2):
                value = flat[end, pl.ds(z * ROWS + x, RHS, stride=CELLS), :]
                for shift, moved in enumerate(three(value)):
                    start_ref[shift, x, z, end] = moved
    for x in range(SENT):
        for end in range(2):
            row = 1 + x
            total = stencil(
                lambda dx, dy, z: start_ref[dy + 1, row + dx, z, end],
                lambda k: spread(weights_ref, (row, end), k),
            )
            for z in range(PLANES):
                for shift, moved in enumerate(three(0.5 * total[z])):
                    first_ref[shift, x, z, end] = moved
                    if shift == 1:
                        at = (x * PLANES + z) * RHS
                        fresh[end, at : at + RHS, :] = moved
    slot4 = lane // 4
    for end in range(2):
        common = jnp.zeros((8, LANES), F32)
        origin = LANES - 3 if end == 0 else LANES - 1
        for group in range(BLOCK_GROUPS):
            block = fresh[end, 8 * group : 8 * group + 8, :]
            slot = BLOCK_GROUPS + group
            common = jnp.where(slot4 == slot, pltpu.roll(block, (4 * slot - origin) % LANES, 1), common)
        blocks, coefs = [], []
        for skip in (0, 2):
            pack = common
            origin = LANES - 4 if end == 0 else 0
            for group in range(BLOCK_GROUPS):
                x, rest = divmod(group, 2 * PLANES)
                z, half = divmod(rest, 2)
                block = start_ref[1, skip + x, z, end, 8 * half : 8 * half + 8, :]
                pack = jnp.where(slot4 == group, pltpu.roll(block, (4 * group - origin) % LANES, 1), pack)
            blocks.append(pack)
            pack = jnp.zeros((8, LANES), F32)
            origin = LANES - 3 if end == 0 else 0
            for group in range(SENT * ROW_GROUPS):
                x, part = divmod(group, ROW_GROUPS)
                block = weights_ref[skip + x, end, 8 * part : 8 * part + 8, :]
                here = (lane >= 3 * group) & (lane < 3 * group + 3)
                pack = jnp.where(here, pltpu.roll(block, (3 * group - origin) % LANES, 1), pack)
            coefs.append(pack)
        at = CORNER_ROWS * end
        near_ref[at : at + 8, :] = jnp.where(core == 0, blocks[1], blocks[0])
        far_ref[at : at + 8, :] = jnp.where(core == 0, blocks[0], blocks[1])
        near_ref[at + 8 : at + 16, :] = jnp.where(core == 0, coefs[1], coefs[0])
        far_ref[at + 8 : at + 16, :] = jnp.where(core == 0, coefs[0], coefs[1])


def basis_kernel(
    far_ref, far_corner_ref, near_ref, near_corner_ref, start_ref, first_ref, own_weights_ref,
    split_ref, packed_ref,
    sides, corners, basis, side_weights, gram,
):
    core = lax.axis_index("c")
    lane = lane_index((8, LANES))
    wide = lane_index((RHS, LANES))

    def place(near_side, far_side):
        sides[near_side, 0:NEAR_ROWS, :] = near_ref[...]
        sides[far_side, 0:NEAR_ROWS, :] = far_ref[0:NEAR_ROWS, :]
        corners[near_side] = near_corner_ref[...]
        corners[far_side] = far_corner_ref[...]

    @pl.when(core == 0)
    def _():
        place(1, 0)

    @pl.when(core != 0)
    def _():
        place(0, 1)

    def put(step, x, z, end, value):
        if step == STEPS:
            basis[step, 1, x, z, end] = value
            return
        for shift, moved in enumerate(three(value)):
            basis[step, shift, x, z, end] = moved

    def get(step, dy, x, z, end):
        own = x - REACH
        if step == 0 and 0 <= own < ROWS:
            return start_ref[dy + 1, own, z, end]
        if step == 1 and 1 <= own <= 2:
            return first_ref[dy + 1, own - 1, z, end]
        return basis[step, dy + 1, x, z, end]

    def weight(x, end, k):
        own = x - REACH
        if 0 <= own < ROWS:
            return spread(own_weights_ref, (own, end), k)
        side, row = (0, x - 2) if own < 0 else (1, x - REACH - ROWS)
        return spread(side_weights, (side, row, end), k)

    for side in range(2):
        low = packs_of(corners.at[side], 0, 2)
        high = packs_of(corners.at[side], CORNER_ROWS, 2)
        for step in range(2):
            if step == 0:
                places = (LANES - 4, lane >= LANES - 4), (0, lane < 4)
                first = 2 if side == 0 else REACH + ROWS
            else:
                places = (LANES - 3, (lane >= LANES - 3) | (lane == 0)), (LANES - 1, (lane < 3) | (lane == LANES - 1))
                first = 1 if side == 0 else REACH + ROWS + 1
            for x in range(SENT):
                for z in range(PLANES):
                    for half in range(2):
                        slot = step * BLOCK_GROUPS + (x * PLANES + z) * 2 + half
                        block = sides[side, 8 * slot : 8 * slot + 8, :]
                        for end, pack in enumerate((low[0], high[0])):
                            value = patched(block, pack, slot, 4, *places[end])
                            basis[step, 1, first + x, z, end, 8 * half : 8 * half + 8, :] = value
        for x in range(SENT):
            for part in range(ROW_GROUPS):
                slot = x * ROW_GROUPS + part
                at = COEFS_AT + x * USED + 8 * part
                block = sides[side, at : at + 8, :]
                at = slice(8 * part, 8 * part + 8)
                side_weights[side, x, 0, at, :] = patched(block, low[1], slot, 3, LANES - 3, lane >= LANES - 3)
                side_weights[side, x, 1, at, :] = patched(block, high[1], slot, 3, 0, lane < 3)

    for step, rows in ((0, (2, 3, 8, 9)), (1, (1, 2, 9, 10))):
        for x in rows:
            for z in range(PLANES):
                for end in range(2):
                    value = basis[step, 1, x, z, end]
                    basis[step, 0, x, z, end] = pltpu.roll(value, 1, 1)
                    basis[step, 2, x, z, end] = pltpu.roll(value, LANES - 1, 1)

    for step in range(1, STEPS + 1):
        rows = range(step, EXTENT - step) if step > 1 else (3, 4, 7, 8)
        for x in rows:
            for end in range(2):
                total = stencil(
                    lambda dx, dy, z: get(step - 1, dy, x + dx, z, end),
                    lambda k: weight(x, end, k),
                )
                for z in range(PLANES):
                    value = 0.5 * total[z] if step == 1 else total[z] - get(step - 2, 0, x, z, end)
                    put(step, x, z, end, value)

    for step in range(STEPS + 1):
        for x in range(ROWS):
            for z in range(PLANES):
                left, right = (get(step, 0, REACH + x, z, end) for end in range(2))
                value = jnp.where(wide < LANES // 2, left, right)
                rest = value - value.astype(BF16).astype(F32)
                cell = (z * ROWS + x) * LANES
                at = RHS * step
                split_ref[at : at + RHS, cell : cell + LANES] = value.astype(BF16)
                split_ref[2 * WIDTH + at : 2 * WIDTH + at + RHS, cell : cell + LANES] = value.astype(BF16)
                split_ref[WIDTH + at : WIDTH + at + RHS, cell : cell + LANES] = rest.astype(BF16)

    dims = (((1,), (1,)), ((), ()))
    both = split_ref[0 : 2 * WIDTH, :]
    products = lax.dot_general(both, both, dims, preferred_element_type=F32)
    crossed = products[0:WIDTH, WIDTH : 2 * WIDTH] + products[WIDTH : 2 * WIDTH, 0:WIDTH]
    gram[:, 0:WIDTH] = products[0:WIDTH, 0:WIDTH] + crossed
    lane32 = lane_index((32, LANES))
    packed = jnp.where(lane32 < WIDTH, gram[48:80, :], pltpu.roll(gram[16:48, :], WIDTH, 1))
    packed_ref[...] = packed
    packed_ref[0:16, :] = jnp.where(wide < 112, packed[0:16, :], pltpu.roll(gram[0:16, :], 112, 1))


def finish_kernel(cells, packed_ref, split_ref, q_ref, r_ref, square):
    packed = packed_ref[...] * (1.0 / cells)
    square[...] = jnp.zeros((LANES, LANES), F32)
    square[48:80, :] = packed
    square[16:48, :] = pltpu.roll(packed, 48, 1)
    square[0:16, :] = pltpu.roll(packed[0:16, :], 16, 1)
    whole = square[...]
    turned = whole.T
    row = lax.broadcasted_iota(jnp.int32, (LANES, LANES), 0)
    lane = lane_index((LANES, LANES))
    square[...] = jnp.where(lane <= row, whole, turned)
    lane = lane_index((8, LANES))
    inner = lax.broadcasted_iota(jnp.int32, (8, LANES), 0)
    groups = WIDTH // 8
    part = [square[8 * g : 8 * g + 8, :] for g in range(groups)]
    for own in range(groups):
        first = 8 * own
        inside = (lane >= first) & (lane < first + 8)
        rows = [jnp.broadcast_to(part[own][k : k + 1, :], (8, LANES)) for k in range(8)]
        small = {
            (k, l): jnp.broadcast_to(rows[k][:, first + l : first + l + 1], (8, LANES))
            for k in range(8)
            for l in range(k, 8)
        }
        rows = [jnp.where(inside, jnp.where(lane == first + k, 1.0, 0.0), rows[k]) for k in range(8)]
        over, factor = [None] * 8, {}
        for k in range(8):
            over[k] = 1.0 / small[k, k]
            for l in range(k + 1, 8):
                factor[l, k] = small[k, l] * over[k]
                for m in range(l, 8):
                    small[l, m] = small[l, m] - factor[l, k] * small[k, m]
                rows[l] = rows[l] - factor[l, k] * rows[k]
        solved = [None] * 8
        for k in reversed(range(8)):
            solved[k] = rows[k] * over[k]
            for l in range(k + 1, 8):
                solved[k] = solved[k] - factor[l, k] * solved[l]
        for g in range(own + 1, groups):
            total = jnp.where(inside, 0.0, part[g])
            for k in range(8):
                column = jnp.broadcast_to(part[g][:, first + k : first + k + 1], (8, LANES))
                total = total - column * solved[k]
            part[g] = total
        lower, upper = jnp.zeros((8, LANES), F32), jnp.zeros((8, LANES), F32)
        for k in range(8):
            scale = lax.rsqrt(small[k, k])
            lower = jnp.where(inner == k, rows[k] * scale, lower)
            high = rows[k]
            for l in range(k, 8):
                high = jnp.where(lane == first + l, small[k, l], high)
            upper = jnp.where(inner == k, high * scale, upper)
        r_ref[first : first + 8, :] = jnp.where(lane >= inner + first, upper, 0.0)[:, 0:WIDTH]
        square[first : first + 8, :] = jnp.where(lane <= inner + first, lower, 0.0)
    inverse = square[0:WIDTH, 0:WIDTH]
    top = inverse.astype(BF16)
    rest = (inverse - top.astype(F32)).astype(BF16)
    parts = jnp.concatenate([top, top, rest], axis=1)
    for cell in range(0, CELLS, 2):
        block = jnp.dot(parts, split_ref[:, cell * LANES : (cell + 2) * LANES], preferred_element_type=F32)
        q_ref[pl.ds(cell, WIDTH, stride=CELLS), :] = block[:, 0:LANES]
        q_ref[pl.ds(cell + 1, WIDTH, stride=CELLS), :] = block[:, LANES:]


def call(kernel, inputs, shapes, scratch=(), space=pltpu.VMEM, cost=None):
    return pl.pallas_call(
        kernel,
        out_shape=[jax.ShapeDtypeStruct(shape, dtype) for shape, dtype in shapes],
        in_specs=[pl.BlockSpec(memory_space=space)] * inputs,
        out_specs=[pl.BlockSpec(memory_space=pltpu.VMEM)] * len(shapes),
        scratch_shapes=list(scratch),
        cost_estimate=cost,
        compiler_params=pltpu.CompilerParams(vmem_limit_bytes=32 << 20),
    )


def exchange(pieces, axes):
    return lax.all_to_all(pieces, axes, split_axis=0, concat_axis=0, tiled=True)


def summed_everywhere(packed):
    piece = exchange(packed, PLANE).sum(axis=0)
    piece = exchange(jnp.broadcast_to(piece, packed.shape), COLUMN).sum(axis=0)
    return exchange(jnp.broadcast_to(piece, packed.shape), PLANE)


def local(right_sides, coefficients):
    vectors = right_sides.reshape(VECTOR_ROWS, LANES)
    raw = coefficients.reshape(27 * CELLS, LANES)
    across, along = lax.axis_size(GX), lax.axis_size(GY)
    up = [(i, i + 1) for i in range(along - 1)]
    down = [(j, i) for i, j in up]
    near = [(i, i ^ 1) for i in range(across)]
    far = [(i, (i - 1) % across if i % 2 == 0 else (i + 1) % across) for i in range(across)]

    edge = ((EDGE_ROWS, LANES), F32)
    coefs, own, to_far, to_near = call(
        prepare_kernel,
        2,
        [((rows, LANES), F32) for rows in (COEF_ROWS, VECTOR_ROWS, FAR_ROWS, NEAR_ROWS)],
        [
            pltpu.VMEM((27 * CELLS, LANES), F32),
            pltpu.VMEM((3, ROWS, PLANES, RHS, LANES), F32),
            pltpu.SemaphoreType.DMA((2,)),
        ],
        pltpu.HBM,
    )(*[pltpu.with_memory_space_constraint(t, pltpu.HBM) for t in (vectors, raw)])
    from_far = lax.ppermute(to_far, GX, far)
    from_near = lax.ppermute(to_near, GX, near)
    to_up, to_down = call(edge_kernel, 2, [edge, edge])(own, coefs)
    low = lax.ppermute(to_up, GY, up)
    high = lax.ppermute(to_down, GY, down)
    corner = ((2 * CORNER_ROWS, LANES), F32)
    near_corner, far_corner, start, first, weights = call(
        own_kernel,
        4,
        [
            corner,
            corner,
            ((3, ROWS, PLANES, 2, RHS, LANES), F32),
            ((3, SENT, PLANES, 2, RHS, LANES), F32),
            ((ROWS, 2, PER_ROW, LANES), F32),
        ],
        [pltpu.VMEM((2, VECTOR_ROWS, LANES), F32), pltpu.VMEM((2, BLOCK_ROWS, LANES), F32)],
        cost=pl.CostEstimate(flops=10000000000, bytes_accessed=0, transcendentals=0),
    )(own, coefs, low, high)
    far_corner = lax.ppermute(far_corner, GX, far)
    near_corner = lax.ppermute(near_corner, GX, near)
    split, packed = call(
        basis_kernel,
        7,
        [((3 * WIDTH, CELLS * LANES), BF16), ((32, LANES), F32)],
        [
            pltpu.VMEM((2, SIDE_ROWS, LANES), F32),
            pltpu.VMEM((2, 2 * CORNER_ROWS, LANES), F32),
            pltpu.VMEM((STEPS + 1, 3, EXTENT, PLANES, 2, RHS, LANES), F32),
            pltpu.VMEM((2, SENT, 2, PER_ROW, LANES), F32),
            pltpu.VMEM((WIDTH, LANES), F32),
        ],
    )(from_far, far_corner, from_near, near_corner, start, first, weights)
    packed = summed_everywhere(packed)
    cells = CELLS * LANES * across * along
    q, r = call(
        functools.partial(finish_kernel, cells),
        2,
        [((WIDTH * CELLS, LANES), F32), ((WIDTH, WIDTH), F32)],
        [pltpu.VMEM((LANES, LANES), F32)],
    )(packed, split)
    return q.reshape(WIDTH, PLANES, ROWS, LANES), r


def solution(mesh):
    mesh = Mesh(mesh.devices.reshape(4, 4, 2, 8, 4), ("y", "zh", "c", "zl", "x"))
    placed = P(None, None, GX, GY)
    return jax.shard_map(
        local,
        mesh=mesh,
        in_specs=(placed, placed),
        out_specs=(placed, P()),
        check_vma=False,
    )
```

```python
import functools

import jax
import jax.numpy as jnp
from jax import lax
from jax.experimental import pallas as pl
from jax.experimental.pallas import tpu as pltpu
from jax.sharding import Mesh, PartitionSpec as P

STEPS = 4
RHS = 16
WIDTH = RHS * (STEPS + 1)
ROWS = 4
PLANES = 4
LANES = 128
CELLS = ROWS * PLANES
REACH = STEPS

PLANE = ("y", "c", "x")
COLUMN = ("zh", "zl")
GX = ("y", "zh", "c")
GY = ("zl", "x")

FIRST_K = (0 + 9, 0, 0, 0)
LAST_K = (27, 27, 27, 18)
PLANE_AT = (0, 18, 45, 72)
PER_ROW = 96
USED = 90
VECTOR_ROWS = RHS * CELLS
COEF_ROWS = ROWS * PER_ROW
SENT = 2
BLOCK_ROWS = SENT * PLANES * RHS
COEFS_AT = 2 * BLOCK_ROWS
TOWARD = 30
TOWARD_AT = (0, 6, 15, 24)
NEAR_ROWS = COEFS_AT + USED + TOWARD
FAR_ROWS = NEAR_ROWS
SIDE_ROWS = NEAR_ROWS + 12
EDGE_ROWS = 24
CORNER_ROWS = 16
ROW_GROUPS = PER_ROW // 8
VECTOR_GROUPS = VECTOR_ROWS // 8
COEF_GROUPS = ROWS * ROW_GROUPS
BLOCK_GROUPS = BLOCK_ROWS // 8
EXTENT = ROWS + 2 * REACH

F32 = jnp.float32
BF16 = jnp.bfloat16


def lane_index(shape):
    return lax.broadcasted_iota(jnp.int32, shape, 1)


def spread(ref, at, row):
    return ref[(*at, pl.ds(row, 8, stride=0), slice(None))]


def full_row(z, dz, dx, dy):
    return PLANE_AT[z] + 9 * (dz + 1) + 3 * (dx + 1) + (dy + 1) - FIRST_K[z]


def toward_row(z, dz, dx, dy):
    return TOWARD_AT[z] + 3 * (dz if z == 0 else dz + 1) + dy + 1


def keep_toward(read, write, dx):
    for z in range(PLANES):
        for dz in range(-1, 2):
            if 0 <= z + dz < PLANES:
                write(toward_row(z, dz, dx, -1), read(full_row(z, dz, dx, -1)))


def stencil(get, weight, steps=(-1, 0, 1), row_of=full_row):
    total = [None] * PLANES
    for dx in steps:
        for dy in range(-1, 2):
            for source in range(PLANES):
                value = get(dx, dy, source)
                for dz in range(-1, 2):
                    z = source - dz
                    if not 0 <= z < PLANES:
                        continue
                    factor = weight(row_of(z, dz, dx, dy))
                    term = jnp.concatenate([factor, factor], axis=0) * value
                    total[z] = term if total[z] is None else total[z] + term
    return total


def three(value):
    return (pltpu.roll(value, 1, 1), value, pltpu.roll(value, LANES - 1, 1))


def prepare_kernel(v_ref, c_ref, coefs_ref, own_ref, far_ref, near_ref, raw, turned, turned1, partial, toward, sems):
    copies = [
        pltpu.make_async_copy(v_ref, own_ref, sems.at[0]),
        pltpu.make_async_copy(c_ref, raw, sems.at[1]),
    ]
    for copy in copies:
        copy.start()

    core = lax.axis_index("c")
    copies[0].wait()
    for x in range(ROWS):
        for z in range(PLANES):
            value = own_ref[pl.ds(z * ROWS + x, RHS, stride=CELLS), :]
            for shift, moved in enumerate(three(value)):
                turned[shift, x, z] = moved
    copies[1].wait()
    for x in range(ROWS):
        for z in range(PLANES):
            first, count = FIRST_K[z], LAST_K[z] - FIRST_K[z]
            rows = raw[pl.ds(first * CELLS + z * ROWS + x, count, stride=CELLS), :]
            number = first + lax.broadcasted_iota(jnp.int32, rows.shape, 0)
            rows = jnp.where(number == 13, 4.0 * rows - 6.0, 4.0 * rows)
            at = x * PER_ROW + PLANE_AT[z]
            coefs_ref[at : at + count, :] = rows
        at = x * PER_ROW + USED
        coefs_ref[at : at + PER_ROW - USED, :] = jnp.zeros((PER_ROW - USED, LANES), F32)
    for x in range(SENT):
        row = 1 + x
        total = stencil(
            lambda dx, dy, z: turned[dy + 1, row + dx, z],
            lambda k: spread(coefs_ref, (), row * PER_ROW + k),
        )
        for z in range(PLANES):
            for shift, moved in enumerate(three(0.5 * total[z])):
                turned1[shift, x, z] = moved
    for side in range(SENT):
        row, dx = 1 + side, 2 * side - 1
        total = stencil(
            lambda dx, dy, z: turned1[dy + 1, row - 1 + dx, z],
            lambda k: spread(coefs_ref, (), row * PER_ROW + k),
            (0, -dx),
        )
        for z in range(PLANES):
            partial[side, z] = total[z] - turned[1, row, z]

        def write(at, value, side=side):
            toward[side, at : at + 3, :] = value

        keep_toward(lambda at: coefs_ref[row * PER_ROW + at : row * PER_ROW + at + 3, :], write, dx)
    for ref, last in ((near_ref, core == 0), (far_ref, core != 0)):
        side = jnp.where(last, 1, 0)
        for z in range(PLANES):
            for x in range(SENT):
                at = (x * PLANES + z) * RHS
                ref[at : at + RHS, :] = turned[1, 2 * side + x, z]
            at = BLOCK_ROWS + z * RHS
            ref[at : at + RHS, :] = turned1[1, side, z]
            ref[at + BLOCK_ROWS // 2 : at + BLOCK_ROWS // 2 + RHS, :] = partial[side, z]
        start = pl.multiple_of(3 * side * PER_ROW, 8)
        ref[COEFS_AT : COEFS_AT + USED, :] = coefs_ref[pl.ds(start, USED), :]
        ref[COEFS_AT + USED : COEFS_AT + USED + TOWARD, :] = toward[side, 0:TOWARD, :]


def edge_kernel(v_ref, coefs_ref, up_ref, down_ref):
    slot = lane_index((8, LANES)) // 4
    zero = jnp.zeros((8, LANES), F32)
    up, down = [zero] * 3, [zero] * 3
    for group in range(VECTOR_GROUPS + COEF_GROUPS):
        if group < VECTOR_GROUPS:
            block = v_ref[8 * group : 8 * group + 8, :]
        else:
            at = 8 * (group - VECTOR_GROUPS)
            block = coefs_ref[at : at + 8, :]
        pack, place = divmod(group, 32)
        here = slot == place
        up[pack] = jnp.where(here, pltpu.roll(block, (4 * place + 4) % LANES, 1), up[pack])
        down[pack] = jnp.where(here, pltpu.roll(block, (4 * place) % LANES, 1), down[pack])
    for pack in range(3):
        up_ref[8 * pack : 8 * pack + 8, :] = up[pack]
        down_ref[8 * pack : 8 * pack + 8, :] = down[pack]


def patched(block, pack, slot, width, start, mask):
    return jnp.where(mask, pltpu.roll(pack, (start - width * slot) % LANES, 1), block)


def packs_of(ref, at, count):
    return [ref[at + 8 * p : at + 8 * p + 8, :] for p in range(count)]


def own_kernel(
    own_ref, coefs_ref, low_ref, high_ref,
    near_ref, far_ref, start_ref, first_ref, weights_ref,
    flat, partial, toward,
):
    core = lax.axis_index("c")
    lane = lane_index((8, LANES))
    low, high = packs_of(low_ref, 0, 3), packs_of(high_ref, 0, 3)
    for group in range(VECTOR_GROUPS + COEF_GROUPS):
        pack, slot = divmod(group, 32)
        if group < VECTOR_GROUPS:
            block = own_ref[8 * group : 8 * group + 8, :]
        else:
            at = 8 * (group - VECTOR_GROUPS)
            block = coefs_ref[at : at + 8, :]
        ends = (
            patched(block, low[pack], slot, 4, LANES - 4, lane >= LANES - 4),
            patched(block, high[pack], slot, 4, 0, lane < 4),
        )
        for end in range(2):
            if group < VECTOR_GROUPS:
                flat[end, 8 * group : 8 * group + 8, :] = ends[end]
            else:
                x, part = divmod(group - VECTOR_GROUPS, ROW_GROUPS)
                weights_ref[x, end, 8 * part : 8 * part + 8, :] = ends[end]
    for x in range(ROWS):
        for z in range(PLANES):
            for end in range(2):
                value = flat[end, pl.ds(z * ROWS + x, RHS, stride=CELLS), :]
                for shift, moved in enumerate(three(value)):
                    start_ref[shift, x, z, end] = moved
    for x in range(SENT):
        for end in range(2):
            row = 1 + x
            total = stencil(
                lambda dx, dy, z: start_ref[dy + 1, row + dx, z, end],
                lambda k: spread(weights_ref, (row, end), k),
            )
            for z in range(PLANES):
                for shift, moved in enumerate(three(0.5 * total[z])):
                    first_ref[shift, x, z, end] = moved
    for side in range(SENT):
        row, dx = 1 + side, 2 * side - 1
        for end in range(2):
            total = stencil(
                lambda dx, dy, z: first_ref[dy + 1, row - 1 + dx, z, end],
                lambda k: spread(weights_ref, (row, end), k),
                (0, -dx),
            )
            for z in range(PLANES):
                partial[side, end, z] = total[z] - start_ref[1, row, z, end]
            toward[side, end] = jnp.zeros((32, LANES), F32)

            def write(at, value, side=side, end=end):
                toward[side, end, at : at + 3, :] = value

            keep_toward(lambda at: weights_ref[row, end, at : at + 3, :], write, dx)
    slot4 = lane // 4
    for end in range(2):
        blocks, coefs = [], []
        for side in range(SENT):
            pack = jnp.zeros((8, LANES), F32)
            for slot in range(2 * BLOCK_GROUPS):
                kind, rest = divmod(slot, 2 * PLANES)
                z, half = divmod(rest, 2)
                at = slice(8 * half, 8 * half + 8)
                if kind < 2:
                    block, origin = start_ref[1, 2 * side + kind, z, end, at, :], (LANES - 4, 0)[end]
                elif kind == 2:
                    block, origin = first_ref[1, side, z, end, at, :], (LANES - 3, LANES - 1)[end]
                else:
                    block, origin = partial[side, end, z, at, :], LANES - 2
                pack = jnp.where(slot4 == slot, pltpu.roll(block, (4 * slot - origin) % LANES, 1), pack)
            blocks.append(pack)
            pack = jnp.zeros((8, LANES), F32)
            origin = LANES - 3 if end == 0 else 0
            for slot in range(ROW_GROUPS + 4):
                if slot < ROW_GROUPS:
                    block = weights_ref[3 * side, end, 8 * slot : 8 * slot + 8, :]
                else:
                    at = 8 * (slot - ROW_GROUPS)
                    block = toward[side, end, at : at + 8, :]
                here = (lane >= 3 * slot) & (lane < 3 * slot + 3)
                pack = jnp.where(here, pltpu.roll(block, (3 * slot - origin) % LANES, 1), pack)
            coefs.append(pack)
        at = CORNER_ROWS * end
        near_ref[at : at + 8, :] = jnp.where(core == 0, blocks[1], blocks[0])
        far_ref[at : at + 8, :] = jnp.where(core == 0, blocks[0], blocks[1])
        near_ref[at + 8 : at + 16, :] = jnp.where(core == 0, coefs[1], coefs[0])
        far_ref[at + 8 : at + 16, :] = jnp.where(core == 0, coefs[0], coefs[1])


def basis_kernel(
    far_ref, far_corner_ref, near_ref, near_corner_ref, start_ref, first_ref, own_weights_ref,
    split_ref, packed_ref,
    sides, corners, basis, side_weights, side_toward, partial, gram,
):
    core = lax.axis_index("c")
    lane = lane_index((8, LANES))
    wide = lane_index((RHS, LANES))

    def place(near_side, far_side):
        sides[near_side, 0:NEAR_ROWS, :] = near_ref[...]
        sides[far_side, 0:NEAR_ROWS, :] = far_ref[0:NEAR_ROWS, :]
        corners[near_side] = near_corner_ref[...]
        corners[far_side] = far_corner_ref[...]

    @pl.when(core == 0)
    def _():
        place(1, 0)

    @pl.when(core != 0)
    def _():
        place(0, 1)

    def put(step, x, z, end, value):
        if step == STEPS:
            basis[step, 1, x, z, end] = value
            return
        for shift, moved in enumerate(three(value)):
            basis[step, shift, x, z, end] = moved

    def get(step, dy, x, z, end):
        own = x - REACH
        if step == 0 and 0 <= own < ROWS:
            return start_ref[dy + 1, own, z, end]
        if step == 1 and 1 <= own <= 2:
            return first_ref[dy + 1, own - 1, z, end]
        return basis[step, dy + 1, x, z, end]

    def weight(x, end, k):
        own = x - REACH
        if 0 <= own < ROWS:
            return spread(own_weights_ref, (own, end), k)
        return spread(side_weights, (0 if own < 0 else 1, end), k)

    for side in range(2):
        low = packs_of(corners.at[side], 0, 2)
        high = packs_of(corners.at[side], CORNER_ROWS, 2)
        for slot in range(2 * BLOCK_GROUPS):
            kind, rest = divmod(slot, 2 * PLANES)
            z, half = divmod(rest, 2)
            at = slice(8 * half, 8 * half + 8)
            block = sides[side, 8 * slot : 8 * slot + 8, :]
            if kind < 2:
                places = (LANES - 4, lane >= LANES - 4), (0, lane < 4)
            elif kind == 2:
                places = (LANES - 3, (lane >= LANES - 3) | (lane == 0)), (LANES - 1, (lane < 3) | (lane == LANES - 1))
            else:
                places = ((LANES - 2, (lane >= LANES - 2) | (lane < 2)),) * 2
            for end, pack in enumerate((low[0], high[0])):
                value = patched(block, pack, slot, 4, *places[end])
                if kind < 2:
                    basis[0, 1, (2, 8)[side] + kind, z, end, at, :] = value
                elif kind == 2:
                    basis[1, 1, (2, 9)[side], z, end, at, :] = value
                else:
                    partial[side, end, z, at, :] = value
        for slot in range(ROW_GROUPS + 4):
            at = COEFS_AT + 8 * slot if slot < ROW_GROUPS else COEFS_AT + USED + 8 * (slot - ROW_GROUPS)
            block = sides[side, at : at + 8, :]
            ends = (
                patched(block, low[1], slot, 3, LANES - 3, lane >= LANES - 3),
                patched(block, high[1], slot, 3, 0, lane < 3),
            )
            for end in range(2):
                if slot < ROW_GROUPS:
                    side_weights[side, end, 8 * slot : 8 * slot + 8, :] = ends[end]
                else:
                    at = 8 * (slot - ROW_GROUPS)
                    side_toward[side, end, at : at + 8, :] = ends[end]

    for step, rows in ((0, (2, 3, 8, 9)), (1, (2, 9))):
        for x in rows:
            for z in range(PLANES):
                for end in range(2):
                    value = basis[step, 1, x, z, end]
                    basis[step, 0, x, z, end] = pltpu.roll(value, 1, 1)
                    basis[step, 2, x, z, end] = pltpu.roll(value, LANES - 1, 1)

    for step in range(1, STEPS + 1):
        rows = range(step, EXTENT - step) if step > 1 else (3, 4, 7, 8)
        for x in rows:
            for end in range(2):
                if x in (2, 9):
                    side = 0 if x == 2 else 1
                    total = stencil(
                        lambda dx, dy, z: get(step - 1, dy, x + dx, z, end),
                        lambda k: spread(side_toward, (side, end), k),
                        (1 - 2 * side,),
                        toward_row,
                    )
                    for z in range(PLANES):
                        put(step, x, z, end, total[z] + partial[side, end, z])
                    continue
                total = stencil(
                    lambda dx, dy, z: get(step - 1, dy, x + dx, z, end),
                    lambda k: weight(x, end, k),
                )
                for z in range(PLANES):
                    value = 0.5 * total[z] if step == 1 else total[z] - get(step - 2, 0, x, z, end)
                    put(step, x, z, end, value)

    for step in range(STEPS + 1):
        for x in range(ROWS):
            for z in range(PLANES):
                left, right = (get(step, 0, REACH + x, z, end) for end in range(2))
                value = jnp.where(wide < LANES // 2, left, right)
                rest = value - value.astype(BF16).astype(F32)
                cell = (z * ROWS + x) * LANES
                at = RHS * step
                split_ref[at : at + RHS, cell : cell + LANES] = value.astype(BF16)
                split_ref[2 * WIDTH + at : 2 * WIDTH + at + RHS, cell : cell + LANES] = value.astype(BF16)
                split_ref[WIDTH + at : WIDTH + at + RHS, cell : cell + LANES] = rest.astype(BF16)

    dims = (((1,), (1,)), ((), ()))
    both = split_ref[0 : 2 * WIDTH, :]
    products = lax.dot_general(both, both, dims, preferred_element_type=F32)
    crossed = products[0:WIDTH, WIDTH : 2 * WIDTH] + products[WIDTH : 2 * WIDTH, 0:WIDTH]
    gram[:, 0:WIDTH] = products[0:WIDTH, 0:WIDTH] + crossed
    lane32 = lane_index((32, LANES))
    packed = jnp.where(lane32 < WIDTH, gram[48:80, :], pltpu.roll(gram[16:48, :], WIDTH, 1))
    packed_ref[...] = packed
    packed_ref[0:16, :] = jnp.where(wide < 112, packed[0:16, :], pltpu.roll(gram[0:16, :], 112, 1))


def finish_kernel(cells, packed_ref, split_ref, q_ref, r_ref, square):
    packed = packed_ref[...] * (1.0 / cells)
    square[...] = jnp.zeros((LANES, LANES), F32)
    square[48:80, :] = packed
    square[16:48, :] = pltpu.roll(packed, 48, 1)
    square[0:16, :] = pltpu.roll(packed[0:16, :], 16, 1)
    whole = square[...]
    turned = whole.T
    row = lax.broadcasted_iota(jnp.int32, (LANES, LANES), 0)
    lane = lane_index((LANES, LANES))
    square[...] = jnp.where(lane <= row, whole, turned)
    lane = lane_index((8, LANES))
    inner = lax.broadcasted_iota(jnp.int32, (8, LANES), 0)
    groups = WIDTH // 8
    part = [square[8 * g : 8 * g + 8, :] for g in range(groups)]
    for own in range(groups):
        first = 8 * own
        inside = (lane >= first) & (lane < first + 8)
        rows = [jnp.broadcast_to(part[own][k : k + 1, :], (8, LANES)) for k in range(8)]
        small = {
            (k, l): jnp.broadcast_to(rows[k][:, first + l : first + l + 1], (8, LANES))
            for k in range(8)
            for l in range(k, 8)
        }
        rows = [jnp.where(inside, jnp.where(lane == first + k, 1.0, 0.0), rows[k]) for k in range(8)]
        base, factor = [None] * 8, {}
        for k in range(0, 8, 2):
            n = k + 1
            a, b, c = small[k, k], small[k, n], small[n, n]
            over = 1.0 / (a * c - b * b)
            base[k] = (c * rows[k] - b * rows[n]) * over
            base[n] = (a * rows[n] - b * rows[k]) * over
            for l in range(k + 2, 8):
                factor[l, k] = (c * small[k, l] - b * small[n, l]) * over
                factor[l, n] = (a * small[n, l] - b * small[k, l]) * over
            for l in range(k + 2, 8):
                for m in range(l, 8):
                    small[l, m] = small[l, m] - (factor[l, k] * small[k, m] + factor[l, n] * small[n, m])
                rows[l] = rows[l] - (factor[l, k] * rows[k] + factor[l, n] * rows[n])
            ratio = b / a
            for m in range(n, 8):
                small[n, m] = small[n, m] - ratio * small[k, m]
            rows[n] = rows[n] - ratio * rows[k]
        solved = [None] * 8
        for k in reversed(range(8)):
            solved[k] = base[k]
            for l in range(k // 2 * 2 + 2, 8):
                solved[k] = solved[k] - factor[l, k] * solved[l]
        for g in range(own + 1, groups):
            total = jnp.where(inside, 0.0, part[g])
            for k in range(8):
                column = jnp.broadcast_to(part[g][:, first + k : first + k + 1], (8, LANES))
                total = total - column * solved[k]
            part[g] = total
        lower, upper = jnp.zeros((8, LANES), F32), jnp.zeros((8, LANES), F32)
        for k in range(8):
            scale = lax.rsqrt(small[k, k])
            lower = jnp.where(inner == k, rows[k] * scale, lower)
            high = rows[k]
            for l in range(k, 8):
                high = jnp.where(lane == first + l, small[k, l], high)
            upper = jnp.where(inner == k, high * scale, upper)
        r_ref[first : first + 8, :] = jnp.where(lane >= inner + first, upper, 0.0)[:, 0:WIDTH]
        square[first : first + 8, :] = jnp.where(lane <= inner + first, lower, 0.0)
    inverse = square[0:WIDTH, 0:WIDTH]
    top = inverse.astype(BF16)
    rest = (inverse - top.astype(F32)).astype(BF16)
    parts = jnp.concatenate([top, top, rest], axis=1)
    for cell in range(0, CELLS, 2):
        block = jnp.dot(parts, split_ref[:, cell * LANES : (cell + 2) * LANES], preferred_element_type=F32)
        q_ref[pl.ds(cell, WIDTH, stride=CELLS), :] = block[:, 0:LANES]
        q_ref[pl.ds(cell + 1, WIDTH, stride=CELLS), :] = block[:, LANES:]


def call(kernel, inputs, shapes, scratch=(), space=pltpu.VMEM, cost=None):
    return pl.pallas_call(
        kernel,
        out_shape=[jax.ShapeDtypeStruct(shape, dtype) for shape, dtype in shapes],
        in_specs=[pl.BlockSpec(memory_space=space)] * inputs,
        out_specs=[pl.BlockSpec(memory_space=pltpu.VMEM)] * len(shapes),
        scratch_shapes=list(scratch),
        cost_estimate=cost,
        compiler_params=pltpu.CompilerParams(vmem_limit_bytes=32 << 20),
    )


def exchange(pieces, axes):
    return lax.all_to_all(pieces, axes, split_axis=0, concat_axis=0, tiled=True)


def summed_everywhere(packed):
    piece = exchange(packed, PLANE).sum(axis=0)
    piece = exchange(jnp.broadcast_to(piece, packed.shape), COLUMN).sum(axis=0)
    return exchange(jnp.broadcast_to(piece, packed.shape), PLANE)


def local(right_sides, coefficients):
    vectors = right_sides.reshape(VECTOR_ROWS, LANES)
    raw = coefficients.reshape(27 * CELLS, LANES)
    across, along = lax.axis_size(GX), lax.axis_size(GY)
    up = [(i, i + 1) for i in range(along - 1)]
    down = [(j, i) for i, j in up]
    near = [(i, i ^ 1) for i in range(across)]
    far = [(i, (i - 1) % across if i % 2 == 0 else (i + 1) % across) for i in range(across)]

    edge = ((EDGE_ROWS, LANES), F32)
    coefs, own, to_far, to_near = call(
        prepare_kernel,
        2,
        [((rows, LANES), F32) for rows in (COEF_ROWS, VECTOR_ROWS, FAR_ROWS, NEAR_ROWS)],
        [
            pltpu.VMEM((27 * CELLS, LANES), F32),
            pltpu.VMEM((3, ROWS, PLANES, RHS, LANES), F32),
            pltpu.VMEM((3, SENT, PLANES, RHS, LANES), F32),
            pltpu.VMEM((SENT, PLANES, RHS, LANES), F32),
            pltpu.VMEM((SENT, 32, LANES), F32),
            pltpu.SemaphoreType.DMA((2,)),
        ],
        pltpu.HBM,
    )(*[pltpu.with_memory_space_constraint(t, pltpu.HBM) for t in (vectors, raw)])
    from_far = lax.ppermute(to_far, GX, far)
    from_near = lax.ppermute(to_near, GX, near)
    to_up, to_down = call(edge_kernel, 2, [edge, edge])(own, coefs)
    low = lax.ppermute(to_up, GY, up)
    high = lax.ppermute(to_down, GY, down)
    corner = ((2 * CORNER_ROWS, LANES), F32)
    near_corner, far_corner, start, first, weights = call(
        own_kernel,
        4,
        [
            corner,
            corner,
            ((3, ROWS, PLANES, 2, RHS, LANES), F32),
            ((3, SENT, PLANES, 2, RHS, LANES), F32),
            ((ROWS, 2, PER_ROW, LANES), F32),
        ],
        [pltpu.VMEM((2, VECTOR_ROWS, LANES), F32), pltpu.VMEM((2, 2, PLANES, RHS, LANES), F32), pltpu.VMEM((2, 2, 32, LANES), F32)],
        cost=pl.CostEstimate(flops=10000000000, bytes_accessed=0, transcendentals=0),
    )(own, coefs, low, high)
    far_corner = lax.ppermute(far_corner, GX, far)
    near_corner = lax.ppermute(near_corner, GX, near)
    split, packed = call(
        basis_kernel,
        7,
        [((3 * WIDTH, CELLS * LANES), BF16), ((32, LANES), F32)],
        [
            pltpu.VMEM((2, SIDE_ROWS, LANES), F32),
            pltpu.VMEM((2, 2 * CORNER_ROWS, LANES), F32),
            pltpu.VMEM((STEPS + 1, 3, EXTENT, PLANES, 2, RHS, LANES), F32),
            pltpu.VMEM((2, 2, PER_ROW, LANES), F32),
            pltpu.VMEM((2, 2, 32, LANES), F32),
            pltpu.VMEM((2, 2, PLANES, RHS, LANES), F32),
            pltpu.VMEM((WIDTH, LANES), F32),
        ],
    )(from_far, far_corner, from_near, near_corner, start, first, weights)
    packed = summed_everywhere(packed)
    cells = CELLS * LANES * across * along
    q, r = call(
        functools.partial(finish_kernel, cells),
        2,
        [((WIDTH * CELLS, LANES), F32), ((WIDTH, WIDTH), F32)],
        [pltpu.VMEM((LANES, LANES), F32)],
    )(packed, split)
    return q.reshape(WIDTH, PLANES, ROWS, LANES), r


def solution(mesh):
    mesh = Mesh(mesh.devices.reshape(4, 4, 2, 8, 4), ("y", "zh", "c", "zl", "x"))
    placed = P(None, None, GX, GY)
    return jax.shard_map(
        local,
        mesh=mesh,
        in_specs=(placed, placed),
        out_specs=(placed, P()),
        check_vma=False,
    )
```
